32 devices in a mesh: pipe: 8 (over z, core), expert: 4 (over y, x).
Axes of the slice: x: 2, y: 2, z: 4, core: 2. Of those that a mesh axis runs over, the one named last changes fastest.
Arguments:
- fwd_state: bfloat16 [8, 512, 3584], P('pipe', 'expert'), may hold values from -6 to 6
- bwd_cot: bfloat16 [8, 512, 3584], P('pipe', 'expert'), may hold values from -6 to 6
- saved_inputs: bfloat16 [2, 8, 512, 3584], P(None, 'pipe', 'expert'), may hold values from -6 to 6
- fwd_entry: bfloat16 [512, 3584], P('expert'), may hold values from -6 to 6
- bwd_entry: bfloat16 [512, 3584], P('expert'), may hold values from -6 to 6
- fwd_ids: int32 [2, 8, 512, 2], P(None, 'pipe', 'expert'), may hold values from 0 to 3, all different within a row; in each aligned block of 128 rows (0 to 127, 128 to 255, ..., all dimensions but the last counted through in order) at most 80 rows name the same one
- bwd_ids: int32 [2, 8, 512, 2], P(None, 'pipe', 'expert'), may hold values from 0 to 3, all different within a row; in each aligned block of 128 rows (0 to 127, 128 to 255, ..., all dimensions but the last counted through in order) at most 80 rows name the same one
- norm_gain: float32 [8, 3584], P('pipe'), may hold values from 0.1 to 1.9
- router: bfloat16 [8, 3584, 4], P('pipe'), may hold values from -0.09375 to 0.09375
- up_weight: bfloat16 [8, 4, 3584, 1024], P('pipe', 'expert'), may hold values from -0.09375 to 0.09375
- down_weight: bfloat16 [8, 4, 1024, 3584], P('pipe', 'expert'), may hold values from -0.1875 to 0.1875
Outputs:
- fwd_out: bfloat16 [2, 8, 512, 3584], P(None, 'pipe', 'expert')
- bwd_out: bfloat16 [2, 8, 512, 3584], P(None, 'pipe', 'expert')
The draws below stay inside these ranges and needn't reach their ends.
Inputs may be any that keep to these rules, and one draw needn't show every extreme that they name: `fwd_ids`: the 2 ids of a token differ. Within the 128 tokens of one device (aligned blocks), no expert is named by more than 80 tokens, a bound that some block reaches. `bwd_ids`: as for fwd_ids.
All inputs are finite; a program needn't handle non-finite values.
Results may differ from the reference program's by a relative error of at most 0.0059.
Values may be sent and summed in bfloat16 or wider, within the bound.
A program may use at most 128 MiB of HBM per device.

```python
import math
import jax
import jax.numpy as jnp
import numpy as np
from jax import lax

D = 3584
F = 1024
TOPK = 2
TICKS = 2
TOK_DEV = 128
LAYERS = 8
EXPERTS = 4
TOKENS = 512
CAP = 80
N_EXPERT = 4


def steps_of(key, extent, split, least, top_value):
    loudness, own = 1.0, jax.random.fold_in(key, 6)
    for axis_at, blocks in split:
        draws = jnp.exp(jax.random.uniform(jax.random.fold_in(own, axis_at), (blocks,), jnp.float32, least / len(split), top_value / len(split)))
        loudness = loudness * jnp.repeat(draws, extent[axis_at] // blocks).reshape([-1 if axis == axis_at else 1 for axis in range(len(extent))])
    return loudness


def shared_out(key, own, number, rows, count, top, reach, lean):
    order = jax.random.permutation(key, count)
    crowded, common = portions_of(count, rows * top, reach, lean, True), portions_of(count, rows * top, reach, lean, False)
    places = jnp.arange(count)

    def named(sizes, offset_by):
        used = int((sizes > 0).sum())
        fixed = max(1, used // 4)
        shifted = fixed + (places - fixed + offset_by * (used - fixed)) % max(1, count - fixed)
        return jnp.zeros((count,), jnp.int32).at[order[jnp.where(places < fixed, places, shifted)]].set(jnp.asarray(sizes, jnp.int32))

    sizes = jnp.where(number % 4 == 0, named(crowded, number // 4), named(common, number - number // 4 - 1))
    mixed = jax.random.permutation(jax.random.fold_in(own, 3), count)
    donor, taker = mixed[0:count // 2 * 2:2], mixed[1:count // 2 * 2:2]
    room = jnp.minimum(sizes[donor] - 1, reach - sizes[taker]) // 2
    room = jnp.where((donor == order[0]) | (taker == order[0]) | (sizes[taker] == 0), 0, jnp.maximum(room, 0))
    shifted = jax.random.randint(jax.random.fold_in(own, 4), (count // 2,), 0, 1 << 20) % (room + 1)
    sizes = sizes.at[donor].add(-shifted).at[taker].add(shifted)
    labels = jnp.searchsorted(jnp.cumsum(sizes), jnp.arange(rows * top), side="right").astype(jnp.int32)
    grid = labels.reshape(top, rows).T
    grid = grid[jax.random.permutation(jax.random.fold_in(own, 1), rows)]
    offset_by = jax.random.randint(jax.random.fold_in(own, 2), (rows, 1), 0, top)
    return jnp.take_along_axis(grid, (jnp.arange(top)[None, :] + offset_by) % top, axis=1)


def portions_of(count, total, bound, slope, full):
    weights = [(1 << 20) // math.isqrt(rank ** slope) + 1 for rank in range(1, count + 1)]
    largest = bound if full else min(bound, max(-(-total // count), total * weights[0] // sum(weights)))
    least = 1 if total - largest >= count - 1 else 0
    counts, rest = [largest] + [least] * (count - 1), total - largest - least * (count - 1)
    while rest > 0:
        candidates = [i for i in range(1, count) if counts[i] < largest] or [i for i in range(1, count) if counts[i] < bound]
        pool, left = sum([weights[i] for i in candidates]), rest
        for i in candidates:
            more = min(bound - counts[i], max(1, left * weights[i] // pool), rest)
            counts[i] = counts[i] + more
            rest = rest - more
    return np.array(counts)


def gaussian(key, shape, scale, bound, cuts=(), held_as=jnp.bfloat16):
    values = scale * jax.random.normal(key, shape, jnp.float32)
    if cuts:
        values = values * steps_of(key, shape, cuts, -0.22, 0.18)
    return jnp.clip(values, -bound, bound).astype(held_as)


def setup_inputs(seed: int = 0) -> dict:
    streams_of = jax.random.split(jax.random.key(seed), 12)
    fwd_state = gaussian(streams_of[0], (LAYERS, TOKENS, D), 1.0, 6.0, ((0, 8), (1, 4)))
    bwd_cot = gaussian(streams_of[1], (LAYERS, TOKENS, D), 1.0, 6.0, ((0, 8), (1, 4)))
    saved_inputs = gaussian(streams_of[2], (TICKS, LAYERS, TOKENS, D), 1.0, 6.0, ((1, 8), (2, 4)))
    fwd_entry = gaussian(streams_of[3], (TOKENS, D), 1.0, 6.0, ((0, 4),))
    bwd_entry = gaussian(streams_of[4], (TOKENS, D), 1.0, 6.0, ((0, 4),))
    fwd_ids_keys = jax.random.split(jax.random.fold_in(streams_of[5], 1), TICKS * LAYERS * TOKENS // TOK_DEV)
    fwd_ids_turns = jax.random.permutation(jax.random.fold_in(streams_of[5], 3), TICKS * LAYERS * TOKENS // TOK_DEV)
    fwd_ids = jax.vmap(lambda own, number: shared_out(jax.random.fold_in(streams_of[5], 2), own, number, TOK_DEV, EXPERTS, TOPK, CAP, 2))(fwd_ids_keys, fwd_ids_turns).reshape((TICKS, LAYERS, TOKENS, TOPK))
    bwd_ids_keys = jax.random.split(jax.random.fold_in(streams_of[6], 1), TICKS * LAYERS * TOKENS // TOK_DEV)
    bwd_ids_turns = jax.random.permutation(jax.random.fold_in(streams_of[6], 3), TICKS * LAYERS * TOKENS // TOK_DEV)
    bwd_ids = jax.vmap(lambda own, number: shared_out(jax.random.fold_in(streams_of[6], 2), own, number, TOK_DEV, EXPERTS, TOPK, CAP, 2))(bwd_ids_keys, bwd_ids_turns).reshape((TICKS, LAYERS, TOKENS, TOPK))
    norm_gain = jnp.clip(1.0 + 0.18 * jax.random.normal(streams_of[7], (LAYERS, D), jnp.float32), 0.1, 1.9)
    router = gaussian(streams_of[8], (LAYERS, D, EXPERTS), D ** -0.5, 0.09375, ((0, 8),))
    up_weight = gaussian(streams_of[9], (LAYERS, EXPERTS, D, F), D ** -0.5, 0.09375, ((0, 8), (1, 4)))
    down_weight = gaussian(streams_of[10], (LAYERS, EXPERTS, F, D), F ** -0.5, 0.1875, ((0, 8), (1, 4)))
    return dict(fwd_state=fwd_state, bwd_cot=bwd_cot, saved_inputs=saved_inputs, fwd_entry=fwd_entry, bwd_entry=bwd_entry, fwd_ids=fwd_ids, bwd_ids=bwd_ids, norm_gain=norm_gain, router=router, up_weight=up_weight, down_weight=down_weight)


EPSILON = 1e-06

def normalize(activation, gain_row):
    values = activation.astype(jnp.float32)
    inverse_rms = lax.rsqrt(lax.optimization_barrier(jnp.mean(values * values, axis=-1, keepdims=True)) + EPSILON)
    return ((values * inverse_rms * gain_row).astype(jnp.bfloat16), inverse_rms)

def gating(normed, routing, expert_ids):
    logits = jnp.dot(normed, routing, preferred_element_type=jnp.float32)
    probability = jax.nn.sigmoid(logits)
    picked = expert_ids[:, :, None] == jnp.arange(routing.shape[1], dtype=jnp.int32)[None, None, :]
    chosen = lax.optimization_barrier(jnp.sum(jnp.where(picked, probability[:, None, :], 0.0), axis=-1))
    chosen_sum = lax.optimization_barrier(jnp.sum(chosen, axis=-1, keepdims=True))
    return (chosen / chosen_sum, chosen, chosen_sum, picked)

def expert_forward(row_block, up_matrix, down_matrix):
    upward = jnp.dot(row_block, up_matrix, preferred_element_type=jnp.float32)
    hidden = (upward * jax.nn.sigmoid(upward)).astype(jnp.bfloat16)
    return jnp.dot(hidden, down_matrix, preferred_element_type=jnp.float32).astype(jnp.bfloat16)

def expert_backward(row_block, gradients, up_matrix, down_matrix):
    upward = jnp.dot(row_block, up_matrix, preferred_element_type=jnp.float32)
    sigmoid_up = jax.nn.sigmoid(upward)
    hidden = (upward * sigmoid_up).astype(jnp.bfloat16)
    outputs = jnp.dot(hidden, down_matrix, preferred_element_type=jnp.float32).astype(jnp.bfloat16)
    dhidden = lax.dot_general(gradients, down_matrix, (((1,), (1,)), ((), ())), preferred_element_type=jnp.float32)
    dupward = (dhidden * sigmoid_up * (1.0 + upward * (1.0 - sigmoid_up))).astype(jnp.bfloat16)
    dnormed = lax.dot_general(dupward, up_matrix, (((1,), (1,)), ((), ())), preferred_element_type=jnp.float32)
    return (outputs, dnormed.astype(jnp.bfloat16))

def finish_backward(activation, cotangent, inverse_rms, gain_row, routing, gate_weight, chosen, chosen_sum, picked, expert_out, expert_grad):
    cot_values = cotangent.astype(jnp.float32)
    gate_grad = lax.optimization_barrier(jnp.sum(cot_values[:, None, :] * expert_out.astype(jnp.float32), axis=-1))
    chosen_grad = (gate_grad - lax.optimization_barrier(jnp.sum(gate_grad * gate_weight, axis=-1, keepdims=True))) / chosen_sum
    selected_grad = chosen_grad * chosen * (1.0 - chosen)
    logit_grad = lax.optimization_barrier(jnp.sum(jnp.where(picked, selected_grad[:, :, None], 0.0), axis=1))
    router_part = jnp.dot(logit_grad, routing.astype(jnp.float32).T, precision=lax.Precision.HIGHEST)
    norm_grad = lax.optimization_barrier(jnp.sum(expert_grad.astype(jnp.float32), axis=1)) + router_part
    scaled_grad = norm_grad * gain_row
    values = activation.astype(jnp.float32)
    correction = lax.optimization_barrier(jnp.mean(scaled_grad * values, axis=-1, keepdims=True))
    result = cot_values + inverse_rms * scaled_grad - values * inverse_rms ** 3 * correction
    return result.astype(jnp.bfloat16)

def reference(fwd_state, bwd_cot, saved_inputs, fwd_entry, bwd_entry, fwd_ids, bwd_ids, norm_gain, router, up_weight, down_weight):
    per_expert = N_EXPERT * CAP
    assignments = TOKENS * TOPK
    token_of = jnp.arange(assignments, dtype=jnp.int32) // TOPK

    def route_rows(expert_ids):
        flattened = expert_ids.reshape(assignments)
        onehot = (flattened[:, None] == jnp.arange(EXPERTS, dtype=jnp.int32)[None, :]).astype(jnp.int32)
        position = lax.optimization_barrier(jnp.sum((jnp.cumsum(onehot, axis=0) - 1) * onehot, axis=1))
        return (flattened * per_expert + position).astype(jnp.int32)

    def scatter_rows(rows, slot_index):
        buffer = jnp.zeros((EXPERTS * per_expert, D), jnp.bfloat16).at[slot_index].set(rows)
        return buffer.reshape(EXPERTS, per_expert, D)

    def layer_forward(operands):
        activation, gain_row, routing, up_matrix, down_matrix, expert_ids = operands
        normed, inverse_rms = normalize(activation, gain_row)
        gate_weight, chosen, chosen_sum, picked = gating(normed, routing, expert_ids)
        slot_index = route_rows(expert_ids)
        buffer = scatter_rows(normed[token_of], slot_index)
        results = lax.map(lambda parts: expert_forward(parts[0], parts[1], parts[2]), (buffer, up_matrix, down_matrix))
        expert_out = results.reshape(EXPERTS * per_expert, D)[slot_index].reshape(TOKENS, TOPK, D)
        mixed = activation.astype(jnp.float32) + lax.optimization_barrier(jnp.sum(gate_weight[:, :, None] * expert_out.astype(jnp.float32), axis=1))
        return mixed.astype(jnp.bfloat16)

    def layer_backward(operands):
        activation, cotangent, gain_row, routing, up_matrix, down_matrix, expert_ids = operands
        normed, inverse_rms = normalize(activation, gain_row)
        gate_weight, chosen, chosen_sum, picked = gating(normed, routing, expert_ids)
        out_grad = (gate_weight[:, :, None] * cotangent.astype(jnp.float32)[:, None, :]).astype(jnp.bfloat16)
        slot_index = route_rows(expert_ids)
        row_buffer = scatter_rows(normed[token_of], slot_index)
        grad_buffer = scatter_rows(out_grad.reshape(assignments, D), slot_index)
        outputs, dnormed = lax.map(lambda parts: expert_backward(parts[0], parts[1], parts[2], parts[3]), (row_buffer, grad_buffer, up_matrix, down_matrix))
        expert_out = outputs.reshape(EXPERTS * per_expert, D)[slot_index].reshape(TOKENS, TOPK, D)
        expert_grad = dnormed.reshape(EXPERTS * per_expert, D)[slot_index].reshape(TOKENS, TOPK, D)
        return finish_backward(activation, cotangent, inverse_rms, gain_row, routing, gate_weight, chosen, chosen_sum, picked, expert_out, expert_grad)
    forward_in = fwd_state
    cotangent_in = bwd_cot
    forward_list = []
    backward_list = []
    for tick_number in range(TICKS):
        forward_result = lax.map(layer_forward, (forward_in, norm_gain, router, up_weight, down_weight, fwd_ids[tick_number]))
        backward_result = lax.map(layer_backward, (saved_inputs[tick_number], cotangent_in, norm_gain, router, up_weight, down_weight, bwd_ids[tick_number]))
        forward_list.append(forward_result)
        backward_list.append(backward_result)
        forward_in = jnp.concatenate([fwd_entry[None], forward_result[:-1]], axis=0)
        cotangent_in = jnp.concatenate([backward_result[1:], bwd_entry[None]], axis=0)
    return (jnp.stack(forward_list), jnp.stack(backward_list))
```

```python
import functools

import jax
import jax.numpy as jnp
from jax import lax
from jax.experimental import pallas as pl
from jax.experimental.pallas import tpu as pltpu
from jax.sharding import PartitionSpec as P

EPSILON = 1e-06
LANES = 128
F32 = jnp.float32
BF16 = jnp.bfloat16
I32 = jnp.int32
NN = (((1,), (0,)), ((), ()))
NT = (((1,), (1,)), ((), ()))


def mm(a, b, dims=NN, precision=None):
    return lax.dot_general(a, b, dims, preferred_element_type=F32, precision=precision)


def tile_of(extent, most):
    size = most
    while extent % size:
        size -= LANES
    return size


def sides(experts):
    inner = 2 if experts % 2 == 0 else 1
    return inner, experts // inner


def hops_of(experts):
    inner, outer = sides(experts)
    return ((0, 1), (1, 0)) if inner == outer else ((0, 1), (0, 1))


def near_count(experts):
    extent = sides(experts)
    return sum(extent[first] - 1 for first, _ in hops_of(experts))


def far_count(experts):
    extent = sides(experts)
    return sum((extent[second] - 1) * extent[first] for first, second in hops_of(experts))


def copy_count(experts, ticks):
    near, far = near_count(experts), far_count(experts)
    return ticks * (7 * near + 5 * far + experts - 1) + near


def window_kernel(
    sections,
    experts,
    capacity,
    fwd_state,
    bwd_cot,
    saved,
    fwd_entry,
    bwd_entry,
    fwd_ids,
    bwd_ids,
    gain,
    router,
    up_hbm,
    down_hbm,
    fwd_out,
    bwd_out,
    up_w,
    down_w,
    acts,
    cots,
    stored,
    norm_f,
    norm_s,
    dense_f,
    dense_s,
    dense_c,
    send_f,
    send_s,
    send_c,
    recv_f,
    recv_s,
    recv_c,
    ret_f,
    ret_g,
    part_f,
    part_g,
    comb_f,
    comb_g,
    ids_all,
    gates_all,
    picks,
    stack_f,
    stack_g,
    gate_send,
    gate_ret,
    routing,
    up_buf,
    hid_buf,
    dup_buf,
    scaled_buf,
    load_sems,
    send_sems,
    recv_sems,
    pipe_send,
    pipe_recv,
    out_sems,
):
    ticks, tokens, width = saved.shape
    half = width // 2
    top_count = fwd_ids.shape[1]
    hidden_width = up_w.shape[1]
    rows = experts * capacity
    section = lax.axis_index("pipe")
    me = lax.axis_index("expert")
    extent = sides(experts)
    inner, outer = extent
    hops = hops_of(experts)
    lo, hi = lax.rem(me, inner), lax.div(me, inner)
    wide = tile_of(half, 256)
    wide_count = half // wide
    narrow = tile_of(hidden_width, 256)
    narrow_count = hidden_width // narrow

    def half_at(h):
        return slice(h * half, (h + 1) * half)

    def load_rows(source, target, first):
        return [
            pltpu.make_async_copy(
                source.at[:, half_at(h)], target.at[h], load_sems.at[first + h]
            )
            for h in range(2)
        ]

    load_cot = load_rows(bwd_cot, cots.at[0], 0)
    load_act = load_rows(fwd_state, acts.at[0], 2)
    load_up = pltpu.make_async_copy(up_hbm, up_w, load_sems.at[4])
    load_down = pltpu.make_async_copy(down_hbm, down_w, load_sems.at[5])
    load_stored = [load_rows(saved.at[t], stored.at[t], 10 + 2 * t) for t in range(ticks)]
    for load in [*load_cot, *load_stored[0], *load_act, load_up, load_down]:
        load.start()
    for loads in load_stored[1:]:
        for load in loads:
            load.start()

    barrier = pltpu.get_barrier_semaphore()
    for offset in range(1, experts):
        pl.semaphore_signal(
            barrier,
            inc=1,
            device_id=(section, lax.rem(me + offset, experts)),
            device_id_type=pl.DeviceIdType.MESH,
        )
    for offset in (1, sections - 1):
        pl.semaphore_signal(
            barrier,
            inc=1,
            device_id=(lax.rem(section + offset, sections), me),
            device_id_type=pl.DeviceIdType.MESH,
        )

    counter = iter(range(send_sems.shape[0]))

    def remote(source, target, where):
        index = next(counter)
        copy = pltpu.make_async_remote_copy(
            src_ref=source,
            dst_ref=target,
            send_sem=send_sems.at[index],
            recv_sem=recv_sems.at[index],
            device_id=where,
            device_id_type=pl.DeviceIdType.MESH,
        )
        copy.start()
        return copy

    def device(a, b):
        across = lax.rem(hi + b + outer, outer)
        return (section, across * inner + lax.rem(lo + a + inner, inner))

    def along(axis, offset):
        return device(offset, 0) if axis == 0 else device(0, offset)

    def slot_of(h, j):
        return h * (extent[hops[0][0]] - 1) + j - 1

    def block_of(h, m, j):
        a, b = (m, j) if hops[h][0] else (j, m)
        return b * inner + a

    def block_rows(h, m, j):
        block = block_of(h, m, j)
        return slice(block * capacity, (block + 1) * capacity)

    def ret_rows(h, j, m):
        block = j * extent[hops[h][1]] + m
        return slice(block * capacity, (block + 1) * capacity)

    def ret_span(h, j):
        size = extent[hops[h][1]] * capacity
        return slice(j * size, (j + 1) * size)

    def pick_rows(h, j):
        size = extent[hops[h][1]] * capacity
        return slice(h * rows + j * size, h * rows + (j + 1) * size)

    def send_index(h, m, j):
        skipped = (extent[hops[0][1]] - 1) * extent[hops[0][0]]
        return h * skipped + (m - 1) * extent[hops[h][0]] + j

    def stack_index(h, j):
        return h * extent[hops[0][0]] + j

    def sources(h):
        return range(extent[hops[h][0]])

    def targets(h):
        return range(1, extent[hops[h][1]])

    def relayed(h):
        return range(1, extent[hops[h][0]])

    def waited(copies):
        for copy in copies:
            copy.wait()

    def arrived(copies):
        for copy in copies:
            copy.wait_recv()

    def sent(copies):
        for copy in copies:
            copy.wait_send()

    def wide_at(step):
        return pl.ds(pl.multiple_of(step * wide, LANES), wide)

    def full_at(h, step):
        return pl.ds(pl.multiple_of(h * half + step * wide, LANES), wide)

    def narrow_at(step):
        return pl.ds(pl.multiple_of(step * narrow, LANES), narrow)

    def folded(value):
        return sum(value[:, i : i + LANES] for i in range(0, value.shape[1], LANES))

    def over_wide(h, body, carry=0):
        return lax.fori_loop(0, wide_count, functools.partial(body, h), carry)

    before = lax.broadcasted_iota(I32, (tokens, tokens), 0)
    after = lax.broadcasted_iota(I32, (tokens, tokens), 1)
    upper = jnp.where(before < after, 1.0, 0.0).astype(BF16)
    level = lax.broadcasted_iota(I32, (16, tokens), 0)

    def names_along(axis):
        if axis == 0:
            named = hi * inner + lax.rem(lo + level, inner)
        else:
            named = lax.rem(hi + level, outer) * inner + lo
        return jnp.where(level < extent[axis], named, -1)

    def names_around():
        across = lax.rem(hi + lax.div(level, inner), outer)
        named = across * inner + lax.rem(lo + lax.rem(level, inner), inner)
        return jnp.where(level < experts, named, -1)

    def slots_of(ids, names, step):
        member = sum(jnp.where(ids[k : k + 1] == names, 1.0, 0.0) for k in range(top_count))
        position = mm(member.astype(BF16), upper)
        base = level.astype(F32) * float(step)
        return jnp.where(member > 0.5, position + base, -1.0)

    def placed(slot, count, weight=None):
        line = lax.broadcasted_iota(I32, (count * capacity, tokens), 0).astype(F32)
        return sum(
            jnp.where(
                line == slot[m : m + 1, :], 1.0 if weight is None else weight[m : m + 1, :], 0.0
            )
            for m in range(count)
        )

    def ids_of(direction, tick, h, j):
        return ids_all[0 if j == 0 else 1 + slot_of(h, j), direction * ticks + tick]

    def make_picks(direction, tick):
        for h in range(2):
            second = hops[h][1]
            for j in sources(h):
                slot = slots_of(ids_of(direction, tick, h, j), names_along(second), capacity)
                picks[direction, tick, pick_rows(h, j), :] = placed(slot, extent[second]).astype(
                    BF16
                )

    def make_stacks(direction, tick, stack):
        for h in range(2):
            second = hops[h][1]
            count = extent[second]
            for j in sources(h):
                ids = ids_of(direction, tick, h, j)
                gates = gates_all[direction, tick, 0 if j == 0 else 1 + slot_of(h, j)]
                names = names_along(second)
                slot = slots_of(ids, names, capacity)
                weight = sum(
                    jnp.where(ids[k : k + 1] == names, gates[k : k + 1], 0.0)
                    for k in range(top_count)
                )
                matrix = placed(slot, count, weight).T
                high = matrix.astype(BF16)
                low = (matrix - high.astype(F32)).astype(BF16)
                at = stack_index(h, j)
                stack[at, 0:tokens, 0 : count * capacity] = high
                stack[at, tokens : 2 * tokens, 0 : count * capacity] = low

    def mixed(stack, ret, h, j, at):
        size = extent[hops[h][1]] * capacity
        both = mm(stack[stack_index(h, j), :, 0:size], ret[h, ret_span(h, j), at])
        return both[:tokens] + both[tokens:]

    def inverse_of(act):
        def body(h, step, total):
            values = act[h, :, wide_at(step)].astype(F32)
            return total + folded(values * values)

        total = jnp.zeros((tokens, LANES), F32)
        for h in range(2):
            total = over_wide(h, body, total)
        mean = jnp.sum(total, axis=-1, keepdims=True) / float(width)
        return lax.rsqrt(mean + EPSILON)

    def normalize(act, target):
        inverse = inverse_of(act)

        def body(h, step, logits):
            at, full = wide_at(step), full_at(h, step)
            normed = (act[h, :, at].astype(F32) * inverse * gain[:, full]).astype(BF16)
            target[h, :, at] = normed
            return logits + mm(routing[:, full], normed, NT)

        logits = jnp.zeros((16, tokens), F32)
        for h in range(2):
            logits = over_wide(h, body, logits)
        return inverse, logits

    def gating(direction, tick, logits):
        ids = ids_all[0, direction * ticks + tick]
        probability = jax.nn.sigmoid(logits)
        chosen = [
            jnp.sum(jnp.where(ids[k : k + 1] == level, probability, 0.0), axis=0, keepdims=True)
            for k in range(top_count)
        ]
        total = sum(chosen)
        gates = [value / total for value in chosen]
        gates_all[direction, tick, 0] = jnp.zeros((8, tokens), F32)
        for k in range(top_count):
            gates_all[direction, tick, 0, k : k + 1, :] = gates[k]
        return chosen, total, gates

    def spread(source, target):
        copies = {}
        for h in range(2):
            for j in relayed(h):
                copies[h, j] = remote(
                    source(h), target(slot_of(h, j)), along(hops[h][0], j)
                )
        return copies

    def send_dense(source, dense):
        return spread(lambda h: source.at[h], lambda slot: dense.at[slot])

    def send_gates(direction, tick):
        held = gates_all.at[direction, tick]
        return spread(lambda h: held.at[0], lambda slot: held.at[1 + slot])

    def pack(direction, tick, h, j, source, send, recv):
        pick = picks[direction, tick, pick_rows(h, j), :]
        count = extent[hops[h][1]]

        def body(h, step, carry):
            at = wide_at(step)
            moved = mm(pick, source[:, at]).astype(BF16)
            for m in range(count):
                part = moved[m * capacity : (m + 1) * capacity]
                if m:
                    send[send_index(h, m, j), :, at] = part
                else:
                    recv[h, block_rows(h, 0, j), at] = part
            return carry

        over_wide(h, body)
        return [
            remote(
                send.at[send_index(h, m, j)],
                recv.at[h, block_rows(h, m, j)],
                along(hops[h][1], m),
            )
            for m in targets(h)
        ]

    def pack_own(direction, tick, source, send, recv):
        copies = []
        for h in range(2):
            copies += pack(direction, tick, h, 0, source.at[h], send, recv)
        return copies

    def pack_relayed(direction, tick, dense, trips, send, recv):
        copies = []
        for h in range(2):
            for j in relayed(h):
                trips[h, j].wait_recv()
                copies += pack(direction, tick, h, j, dense.at[slot_of(h, j)], send, recv)
        return copies

    def give_back(block, ret, product):
        trips = {}
        for h in range(2):

            def body(h, step, carry):
                at = wide_at(step)
                value = product(h, step)
                block[h, :, at] = value
                for j in sources(h):
                    ret[h, ret_rows(h, j, 0), at] = value[block_rows(h, 0, j)]
                return carry

            over_wide(h, body)
            for j in reversed(sources(h)):
                trips[h, j] = [
                    remote(
                        block.at[h, block_rows(h, m, j)],
                        ret.at[h, ret_rows(h, j, m)],
                        along(hops[h][1], -m),
                    )
                    for m in targets(h)
                ]
        return trips

    def project(block, at):
        return mm(block[0], up_w[0:half, at]) + mm(block[1], up_w[half:width, at])

    def expert_forward(block):
        def up_body(step, carry):
            at = narrow_at(step)
            upward = project(block, at)
            hid_buf[:, at] = (upward * jax.nn.sigmoid(upward)).astype(BF16)
            return carry

        lax.fori_loop(0, narrow_count, up_body, 0)

        def product(h, step):
            return mm(hid_buf[...], down_w[:, full_at(h, step)]).astype(BF16)

        return give_back(block, ret_f, product)

    def expert_up(block):
        def body(step, carry):
            at = narrow_at(step)
            up_buf[:, at] = project(block, at)
            return carry

        lax.fori_loop(0, narrow_count, body, 0)

    def expert_backward(block, cot_block, tick):
        def body(step, total):
            at = narrow_at(step)
            grad = mm(cot_block[0], down_w[at, 0:half], NT)
            grad = grad + mm(cot_block[1], down_w[at, half:width], NT)
            upward = up_buf[:, at]
            gate = jax.nn.sigmoid(upward)
            hidden = (upward * gate).astype(BF16).astype(F32)
            dup_buf[:, at] = (grad * gate * (1.0 + upward * (1.0 - gate))).astype(BF16)
            return total + folded(hidden * grad)

        total = lax.fori_loop(0, narrow_count, body, jnp.zeros((rows, LANES), F32))
        ones = jnp.ones((8, LANES), F32)
        trips = []
        for source in range(experts):
            part = total[source * capacity : (source + 1) * capacity]
            target = gate_send if source else gate_ret
            target[tick, source] = jnp.zeros((8, LANES), F32)
            target[tick, source, :, 0:capacity] = mm(ones, part, NT, lax.Precision.HIGHEST)
            if source:
                trips.append(
                    remote(
                        gate_send.at[tick, source],
                        gate_ret.at[tick, source],
                        device(-(source % inner), -(source // inner)),
                    )
                )

        def product(h, step):
            return mm(dup_buf[...], up_w[full_at(h, step), :], NT).astype(BF16)

        return trips, give_back(block, ret_g, product)

    def combine(stack, ret, part, comb, trips):
        copies = {}
        for h in range(2):
            for j in relayed(h):
                arrived(trips[h, j])
                slot = slot_of(h, j)

                def body(h, step, carry, j=j, slot=slot):
                    at = wide_at(step)
                    part[slot, :, at] = mixed(stack, ret, h, j, at).astype(BF16)
                    return carry

                over_wide(h, body)
                copies[h, j] = remote(part.at[slot], comb.at[slot], along(hops[h][0], -j))
        for h in range(2):
            arrived(trips[h, 0])
        return copies

    def gathered(stack, ret, comb, h, at):
        total = mixed(stack, ret, h, 0, at)
        for j in relayed(h):
            total = total + comb[slot_of(h, j), :, at].astype(F32)
        return total

    def finish_forward(act, h, trips):
        arrived([trips[h, j] for j in relayed(h)])

        def body(h, step, carry):
            at = wide_at(step)
            total = act[h, :, at].astype(F32) + gathered(stack_f, ret_f, comb_f, h, at)
            act[h, :, at] = total.astype(BF16)
            return carry

        over_wide(h, body)

    def logit_grads(tick, ready):
        chosen, total, gates = ready
        ids = ids_all[0, ticks + tick]
        names = names_around()
        slot = slots_of(ids, names, 0)
        line = lax.broadcasted_iota(I32, (LANES, tokens), 0).astype(F32)
        found = [jnp.zeros((1, tokens), F32) for _ in range(top_count)]
        for source in range(experts):
            spot = jnp.where(line == slot[source : source + 1], 1.0, 0.0)
            value = mm(gate_ret[tick, source], spot, NN, lax.Precision.HIGHEST)[0:1]
            for k in range(top_count):
                found[k] = found[k] + jnp.where(
                    ids[k : k + 1] == names[source : source + 1], value, 0.0
                )
        mean = sum(found[k] * gates[k] for k in range(top_count))
        grads = jnp.zeros((16, tokens), F32)
        for k in range(top_count):
            value = (found[k] - mean) / total * chosen[k] * (1.0 - chosen[k])
            grads = grads + jnp.where(ids[k : k + 1] == level, value, 0.0)
        return jnp.concatenate([grads, jnp.zeros((LANES - 16, tokens), F32)], axis=0).T

    def finish_backward(cot, source, inverse, logit_grad, trips):
        def body(h, step, total):
            at, full = wide_at(step), full_at(h, step)
            grad = gathered(stack_g, ret_g, comb_g, h, at)
            routed = routing[:, full].astype(F32)
            for e in range(experts):
                grad = grad + logit_grad[:, e : e + 1] * routed[e : e + 1, :]
            scaled = grad * gain[:, full]
            scaled_buf[h, :, at] = scaled
            return total + folded(scaled * source[h, :, at].astype(F32))

        total = jnp.zeros((tokens, LANES), F32)
        for h in range(2):
            arrived([trips[h, j] for j in relayed(h)])
            total = over_wide(h, body, total)
        correction = jnp.sum(total, axis=-1, keepdims=True) / float(width)
        factor = inverse * inverse * inverse * correction

        def last_body(h, step, carry):
            at = wide_at(step)
            values = source[h, :, at].astype(F32)
            result = cot[h, :, at].astype(F32) + inverse * scaled_buf[h, :, at] - values * factor
            cot[h, :, at] = result.astype(BF16)
            return carry

        return last_body

    def hop(source, target, entry, tick, direction, h):
        shift = 1 if direction == 0 else -1
        index = 2 * direction + h
        edge = 0 if direction == 0 else sections - 1
        last = sections - 1 - edge
        where = jnp.clip(section + shift, 0, sections - 1)
        copy = pltpu.make_async_remote_copy(
            src_ref=source.at[h],
            dst_ref=target.at[h],
            send_sem=pipe_send.at[tick, index],
            recv_sem=pipe_recv.at[tick, index],
            device_id=(where, me),
            device_id_type=pl.DeviceIdType.MESH,
        )
        fresh = pltpu.make_async_copy(
            entry.at[:, half_at(h)], target.at[h], load_sems.at[6 + index]
        )
        pl.when(section != last)(copy.start)
        pl.when(section == edge)(fresh.start)

        def landed():
            pl.when(section != edge)(copy.wait_recv)
            pl.when(section == edge)(fresh.wait)

        def left():
            pl.when(section != last)(copy.wait_send)

        return landed, left

    for tick in range(ticks):
        for direction, ids in enumerate((fwd_ids, bwd_ids)):
            ids_all[0, direction * ticks + tick] = jnp.full((8, tokens), -1, I32)
            ids_all[0, direction * ticks + tick, 0:top_count, :] = ids[tick]
    routing[...] = jnp.zeros(routing.shape, BF16)
    routing[0:experts, :] = router[...]

    waited(load_cot)
    pl.semaphore_wait(barrier, experts + 1)
    trip_i = spread(lambda h: ids_all.at[0], lambda slot: ids_all.at[1 + slot])
    trip_c = send_dense(cots.at[0], dense_c)
    waited(load_stored[0])
    inverse_s, logits_s = normalize(stored.at[0], norm_s.at[0])
    trip_s = send_dense(norm_s.at[0], dense_s.at[0])
    ready_s = gating(1, 0, logits_s)
    trip_v = send_gates(1, 0)
    waited(load_act)
    _, logits_f = normalize(acts.at[0], norm_f)
    trip_f = send_dense(norm_f, dense_f)
    gating(0, 0, logits_f)
    trip_w = send_gates(0, 0)
    arrived(trip_i.values())
    make_picks(1, 0)
    make_picks(0, 0)
    pack_f = pack_own(0, 0, norm_f, send_f, recv_f.at[0])
    pack_c = pack_own(1, 0, cots.at[0], send_c, recv_c)
    pack_s = pack_own(1, 0, norm_s.at[0], send_s, recv_s.at[0])
    pack_c += pack_relayed(1, 0, dense_c, trip_c, send_c, recv_c)
    pack_s += pack_relayed(1, 0, dense_s.at[0], trip_s, send_s, recv_s.at[0])
    pack_f += pack_relayed(0, 0, dense_f, trip_f, send_f, recv_f.at[0])
    waited([load_up, load_down])

    outs = []
    for tick in range(ticks):
        more = tick + 1 < ticks
        act, cot = acts.at[tick], cots.at[tick]
        inverse, ready = inverse_s, ready_s
        trip_gs = trip_v
        if more:
            waited(load_stored[tick + 1])
            inverse_s, logits_s = normalize(stored.at[tick + 1], norm_s.at[tick + 1])
            next_s = send_dense(norm_s.at[tick + 1], dense_s.at[tick + 1])
            ready_s = gating(1, tick + 1, logits_s)
            trip_v = send_gates(1, tick + 1)
            make_picks(1, tick + 1)
            make_picks(0, tick + 1)
        arrived(trip_w.values())
        make_stacks(0, tick, stack_f)
        arrived(trip_gs.values())
        make_stacks(1, tick, stack_g)

        arrived(pack_f)
        back_f = expert_forward(recv_f.at[tick])
        arrived(pack_s)
        expert_up(recv_s.at[tick])
        arrived(pack_c)
        trip_x, back_g = expert_backward(recv_s.at[tick], recv_c, tick)
        sent(pack_s)
        if more:
            pack_s = pack_own(1, tick + 1, norm_s.at[tick + 1], send_s, recv_s.at[tick + 1])
            pack_s += pack_relayed(
                1, tick + 1, dense_s.at[tick + 1], next_s, send_s, recv_s.at[tick + 1]
            )

        home_f = combine(stack_f, ret_f, part_f, comb_f, back_f)
        home_g = combine(stack_g, ret_g, part_g, comb_g, back_g)

        hops_f = []
        for h in range(2):
            finish_forward(act, h, home_f)
            if more:
                hops_f.append(hop(act, acts.at[tick + 1], fwd_entry, tick, 0, h))
            outs.append(
                pltpu.make_async_copy(
                    act.at[h], fwd_out.at[tick, :, half_at(h)], out_sems.at[tick, h]
                )
            )
            outs[-1].start()
        sent(trip_f.values())
        sent(pack_f)
        sent(trip_w.values())

        arrived(trip_x)
        logit_grad = logit_grads(tick, ready)
        last_body = finish_backward(cot, stored.at[tick], inverse, logit_grad, home_g)
        sent(pack_c)
        sent(trip_c.values())
        hops_b = []
        for h in range(2):
            over_wide(h, last_body)
            if more:
                hops_b.append(hop(cot, cots.at[tick + 1], bwd_entry, tick, 1, h))
            outs.append(
                pltpu.make_async_copy(
                    cot.at[h], bwd_out.at[tick, :, half_at(h)], out_sems.at[tick, 2 + h]
                )
            )
            outs[-1].start()
        sent(trip_s.values())
        sent(trip_gs.values())
        sent(trip_x)
        for trips in (back_f, back_g):
            for copies in trips.values():
                sent(copies)
        sent(home_f.values())
        sent(home_g.values())
        if more:
            for landed, _ in hops_f:
                landed()
            _, logits_f = normalize(acts.at[tick + 1], norm_f)
            trip_f = send_dense(norm_f, dense_f)
            gating(0, tick + 1, logits_f)
            trip_w = send_gates(0, tick + 1)
            pack_f = pack_own(0, tick + 1, norm_f, send_f, recv_f.at[tick + 1])
            for landed, _ in hops_b:
                landed()
            trip_c = send_dense(cots.at[tick + 1], dense_c)
            pack_c = pack_own(1, tick + 1, cots.at[tick + 1], send_c, recv_c)
            pack_f += pack_relayed(0, tick + 1, dense_f, trip_f, send_f, recv_f.at[tick + 1])
            pack_c += pack_relayed(1, tick + 1, dense_c, trip_c, send_c, recv_c)
            for _, left in hops_f + hops_b:
                left()
            trip_s = next_s
    sent(trip_i.values())
    for out in outs:
        out.wait()


def per_device(
    fwd_state,
    bwd_cot,
    saved_inputs,
    fwd_entry,
    bwd_entry,
    fwd_ids,
    bwd_ids,
    norm_gain,
    router,
    up_weight,
    down_weight,
):
    sections = lax.axis_size("pipe")
    experts = lax.axis_size("expert")
    ticks, _, tokens, width = saved_inputs.shape
    top_count = fwd_ids.shape[3]
    hidden_width = up_weight.shape[3]
    capacity = -(-(5 * tokens * top_count // (4 * experts)) // 16) * 16
    rows = experts * capacity
    half = width // 2
    inner, outer = sides(experts)
    near, far = near_count(experts), far_count(experts)
    copies = copy_count(experts, ticks)
    anywhere = pl.BlockSpec(memory_space=pl.ANY)
    close = pl.BlockSpec(memory_space=pltpu.VMEM)
    out = jax.ShapeDtypeStruct((ticks, tokens, width), BF16)
    row_block = pltpu.VMEM((2, rows, half), BF16)
    tick_block = pltpu.VMEM((ticks, 2, rows, half), BF16)
    token_block = pltpu.VMEM((2, tokens, half), BF16)
    tick_tokens = pltpu.VMEM((ticks, 2, tokens, half), BF16)
    near_block = pltpu.VMEM((near, tokens, half), BF16)
    far_block = pltpu.VMEM((far, capacity, half), BF16)
    stack_block = pltpu.VMEM((2 + near, 2 * tokens, max(inner, outer) * capacity), BF16)
    forward, backward = pl.pallas_call(
        functools.partial(window_kernel, sections, experts, capacity),
        name="relay_window",
        out_shape=(out, out),
        in_specs=[anywhere] * 5 + [close] * 4 + [anywhere] * 2,
        out_specs=(anywhere, anywhere),
        scratch_shapes=[
            pltpu.VMEM((width, hidden_width), BF16),
            pltpu.VMEM((hidden_width, width), BF16),
            tick_tokens,
            tick_tokens,
            tick_tokens,
            token_block,
            tick_tokens,
            near_block,
            pltpu.VMEM((ticks, near, tokens, half), BF16),
            near_block,
            far_block,
            far_block,
            far_block,
            tick_block,
            tick_block,
            row_block,
            row_block,
            row_block,
            near_block,
            near_block,
            near_block,
            near_block,
            pltpu.VMEM((1 + near, 2 * ticks, 8, tokens), I32),
            pltpu.VMEM((2, ticks, 1 + near, 8, tokens), F32),
            pltpu.VMEM((2, ticks, 2 * rows, tokens), BF16),
            stack_block,
            stack_block,
            pltpu.VMEM((ticks, experts, 8, LANES), F32),
            pltpu.VMEM((ticks, experts, 8, LANES), F32),
            pltpu.VMEM((16, width), BF16),
            pltpu.VMEM((rows, hidden_width), F32),
            pltpu.VMEM((rows, hidden_width), BF16),
            pltpu.VMEM((rows, hidden_width), BF16),
            pltpu.VMEM((2, tokens, half), F32),
            pltpu.SemaphoreType.DMA((10 + 2 * ticks,)),
            pltpu.SemaphoreType.DMA((copies,)),
            pltpu.SemaphoreType.DMA((copies,)),
            pltpu.SemaphoreType.DMA((ticks, 4)),
            pltpu.SemaphoreType.DMA((ticks, 4)),
            pltpu.SemaphoreType.DMA((ticks, 4)),
        ],
        compiler_params=pltpu.CompilerParams(
            collective_id=0, has_side_effects=True, vmem_limit_bytes=63 * 1024 * 1024
        ),
    )(
        fwd_state[0],
        bwd_cot[0],
        saved_inputs[:, 0],
        fwd_entry,
        bwd_entry,
        jnp.swapaxes(fwd_ids[:, 0], 1, 2),
        jnp.swapaxes(bwd_ids[:, 0], 1, 2),
        norm_gain,
        router[0].T,
        up_weight[0, 0],
        down_weight[0, 0],
    )
    return forward[:, None], backward[:, None]


def solution(mesh):
    placed = (
        P("pipe", "expert", None),
        P("pipe", "expert", None),
        P(None, "pipe", "expert", None),
        P("expert", None),
        P("expert", None),
        P(None, "pipe", "expert", None),
        P(None, "pipe", "expert", None),
        P("pipe", None),
        P("pipe", None, None),
        P("pipe", "expert", None, None),
        P("pipe", "expert", None, None),
    )
    return jax.shard_map(
        per_device,
        mesh=mesh,
        in_specs=placed,
        out_specs=(P(None, "pipe", "expert", None), P(None, "pipe", "expert", None)),
        check_vma=False,
    )
```

```python
import functools

import jax
import jax.numpy as jnp
from jax import lax
from jax.experimental import pallas as pl
from jax.experimental.pallas import tpu as pltpu
from jax.sharding import PartitionSpec as P

EPSILON = 1e-06
LANES = 128
F32 = jnp.float32
BF16 = jnp.bfloat16
I32 = jnp.int32
NN = (((1,), (0,)), ((), ()))
NT = (((1,), (1,)), ((), ()))


def mm(a, b, dims=NN, precision=None):
    return lax.dot_general(a, b, dims, preferred_element_type=F32, precision=precision)


def tile_of(extent, most):
    size = most
    while extent % size:
        size -= LANES
    return size


def sides(experts):
    inner = 2 if experts % 2 == 0 else 1
    return inner, experts // inner


def hops_of(experts):
    inner, outer = sides(experts)
    return ((0, 1), (1, 0)) if inner == outer else ((0, 1), (0, 1))


def near_count(experts):
    extent = sides(experts)
    return sum(extent[first] - 1 for first, _ in hops_of(experts))


def far_count(experts):
    extent = sides(experts)
    return sum((extent[second] - 1) * extent[first] for first, second in hops_of(experts))


def copy_count(experts, ticks):
    near, far = near_count(experts), far_count(experts)
    return ticks * (7 * near + 5 * far + experts - 1) + near


def window_kernel(
    sections,
    experts,
    capacity,
    fwd_state,
    bwd_cot,
    saved,
    fwd_entry,
    bwd_entry,
    fwd_ids,
    bwd_ids,
    gain,
    router,
    up_hbm,
    down_hbm,
    fwd_out,
    bwd_out,
    up_w,
    down_w,
    acts,
    cots,
    stored,
    norm_f,
    norm_s,
    dense_f,
    dense_s,
    dense_c,
    send_f,
    send_s,
    send_c,
    recv_f,
    recv_s,
    recv_c,
    ret_f,
    ret_g,
    part_g,
    comb_f,
    comb_g,
    ids_all,
    gates_all,
    picks,
    stack_f,
    stack_g,
    gate_send,
    gate_ret,
    routing,
    up_buf,
    hid_buf,
    held_buf,
    load_sems,
    send_sems,
    recv_sems,
    pipe_send,
    pipe_recv,
):
    ticks, tokens, width = saved.shape
    half = width // 2
    top_count = fwd_ids.shape[1]
    hidden_width = up_w.shape[1]
    rows = experts * capacity
    section = lax.axis_index("pipe")
    me = lax.axis_index("expert")
    extent = sides(experts)
    inner, outer = extent
    hops = hops_of(experts)
    lo, hi = lax.rem(me, inner), lax.div(me, inner)
    wide = tile_of(half, 896)
    wide_count = half // wide
    narrow = tile_of(hidden_width, 256)
    narrow_count = hidden_width // narrow

    def half_at(h):
        return slice(h * half, (h + 1) * half)

    def load_rows(source, target, first):
        return [
            pltpu.make_async_copy(
                source.at[:, half_at(h)], target.at[h], load_sems.at[first + h]
            )
            for h in range(2)
        ]

    load_cot = load_rows(bwd_cot, cots.at[0], 0)
    load_act = load_rows(fwd_state, acts.at[0], 2)
    load_up = pltpu.make_async_copy(up_hbm, up_w, load_sems.at[4])
    load_down = pltpu.make_async_copy(down_hbm, down_w, load_sems.at[5])
    load_stored = [load_rows(saved.at[t], stored.at[t], 10 + 2 * t) for t in range(ticks)]
    for load in [*load_cot, *load_stored[0], *load_act, load_up, load_down]:
        load.start()
    for loads in load_stored[1:]:
        for load in loads:
            load.start()

    barrier = pltpu.get_barrier_semaphore()
    for offset in range(1, experts):
        pl.semaphore_signal(
            barrier,
            inc=1,
            device_id=(section, lax.rem(me + offset, experts)),
            device_id_type=pl.DeviceIdType.MESH,
        )
    for offset in (1, sections - 1):
        pl.semaphore_signal(
            barrier,
            inc=1,
            device_id=(lax.rem(section + offset, sections), me),
            device_id_type=pl.DeviceIdType.MESH,
        )

    counter = iter(range(send_sems.shape[0]))

    def remote(source, target, where):
        index = next(counter)
        copy = pltpu.make_async_remote_copy(
            src_ref=source,
            dst_ref=target,
            send_sem=send_sems.at[index],
            recv_sem=recv_sems.at[index],
            device_id=where,
            device_id_type=pl.DeviceIdType.MESH,
        )
        copy.start()
        return copy

    def device(a, b):
        across = lax.rem(hi + b + outer, outer)
        return (section, across * inner + lax.rem(lo + a + inner, inner))

    def along(axis, offset):
        return device(offset, 0) if axis == 0 else device(0, offset)

    def slot_of(h, j):
        return h * (extent[hops[0][0]] - 1) + j - 1

    def block_of(h, m, j):
        a, b = (m, j) if hops[h][0] else (j, m)
        return b * inner + a

    def block_rows(h, m, j):
        block = block_of(h, m, j)
        return slice(block * capacity, (block + 1) * capacity)

    def ret_rows(h, j, m):
        block = j * extent[hops[h][1]] + m
        return slice(block * capacity, (block + 1) * capacity)

    def ret_span(h, j):
        size = extent[hops[h][1]] * capacity
        return slice(j * size, (j + 1) * size)

    def pick_rows(h, j):
        size = extent[hops[h][1]] * capacity
        return slice(h * rows + j * size, h * rows + (j + 1) * size)

    def send_index(h, m, j):
        skipped = (extent[hops[0][1]] - 1) * extent[hops[0][0]]
        return h * skipped + (m - 1) * extent[hops[h][0]] + j

    def stack_index(h, j):
        return h * extent[hops[0][0]] + j

    def sources(h):
        return range(extent[hops[h][0]])

    def targets(h):
        return range(1, extent[hops[h][1]])

    def relayed(h):
        return range(1, extent[hops[h][0]])

    def waited(copies):
        for copy in copies:
            copy.wait()

    def arrived(copies):
        for copy in copies:
            copy.wait_recv()

    def sent(copies):
        for copy in copies:
            copy.wait_send()

    def wide_at(step):
        return pl.ds(pl.multiple_of(step * wide, LANES), wide)

    def full_at(h, step):
        return pl.ds(pl.multiple_of(h * half + step * wide, LANES), wide)

    def narrow_at(step):
        return pl.ds(pl.multiple_of(step * narrow, LANES), narrow)

    def folded(value):
        return sum(value[:, i : i + LANES] for i in range(0, value.shape[1], LANES))

    def over_wide(h, body, carry=0):
        return lax.fori_loop(0, wide_count, functools.partial(body, h), carry)

    before = lax.broadcasted_iota(I32, (tokens, tokens), 0)
    after = lax.broadcasted_iota(I32, (tokens, tokens), 1)
    upper = jnp.where(before < after, 1.0, 0.0).astype(BF16)
    level = lax.broadcasted_iota(I32, (16, tokens), 0)

    def names_along(axis):
        if axis == 0:
            named = hi * inner + lax.rem(lo + level, inner)
        else:
            named = lax.rem(hi + level, outer) * inner + lo
        return jnp.where(level < extent[axis], named, -1)

    def names_around():
        across = lax.rem(hi + lax.div(level, inner), outer)
        named = across * inner + lax.rem(lo + lax.rem(level, inner), inner)
        return jnp.where(level < experts, named, -1)

    def slots_of(ids, names, step):
        member = sum(jnp.where(ids[k : k + 1] == names, 1.0, 0.0) for k in range(top_count))
        position = mm(member.astype(BF16), upper)
        base = level.astype(F32) * float(step)
        return jnp.where(member > 0.5, position + base, -1.0)

    def placed(slot, count, weight=None):
        line = lax.broadcasted_iota(I32, (count * capacity, tokens), 0).astype(F32)
        return sum(
            jnp.where(
                line == slot[m : m + 1, :], 1.0 if weight is None else weight[m : m + 1, :], 0.0
            )
            for m in range(count)
        )

    def ids_of(direction, tick, h, j):
        return ids_all[0 if j == 0 else 1 + slot_of(h, j), direction * ticks + tick]

    def make_picks(direction, tick):
        for h in range(2):
            second = hops[h][1]
            for j in sources(h):
                slot = slots_of(ids_of(direction, tick, h, j), names_along(second), capacity)
                picks[direction, pick_rows(h, j), :] = placed(slot, extent[second]).astype(
                    BF16
                )

    def make_stacks(direction, tick, stack):
        for h in range(2):
            second = hops[h][1]
            count = extent[second]
            for j in sources(h):
                ids = ids_of(direction, tick, h, j)
                gates = gates_all[direction, tick, 0 if j == 0 else 1 + slot_of(h, j)]
                names = names_along(second)
                slot = slots_of(ids, names, capacity)
                weight = sum(
                    jnp.where(ids[k : k + 1] == names, gates[k : k + 1], 0.0)
                    for k in range(top_count)
                )
                matrix = placed(slot, count, weight).T
                high = matrix.astype(BF16)
                low = (matrix - high.astype(F32)).astype(BF16)
                at = stack_index(h, j)
                stack[at, 0:tokens, 0 : count * capacity] = high
                stack[at, tokens : 2 * tokens, 0 : count * capacity] = low

    def mixed(stack, ret, h, j, at):
        size = extent[hops[h][1]] * capacity
        both = mm(stack[stack_index(h, j), :, 0:size], ret[h, ret_span(h, j), at])
        return both[:tokens] + both[tokens:]

    def inverse_of(act):
        def body(h, step, total):
            values = act[h, :, wide_at(step)].astype(F32)
            return total + folded(values * values)

        total = jnp.zeros((tokens, LANES), F32)
        for h in range(2):
            total = over_wide(h, body, total)
        mean = jnp.sum(total, axis=-1, keepdims=True) / float(width)
        return lax.rsqrt(mean + EPSILON)

    def normalize(act, target):
        inverse = inverse_of(act)

        def body(h, step, logits):
            at, full = wide_at(step), full_at(h, step)
            normed = (act[h, :, at].astype(F32) * inverse * gain[:, full]).astype(BF16)
            target[h, :, at] = normed
            return logits + mm(routing[:, full], normed, NT)

        logits = jnp.zeros((16, tokens), F32)
        for h in range(2):
            logits = over_wide(h, body, logits)
        return inverse, logits

    def gating(direction, tick, logits):
        ids = ids_all[0, direction * ticks + tick]
        probability = jax.nn.sigmoid(logits)
        chosen = [
            jnp.sum(jnp.where(ids[k : k + 1] == level, probability, 0.0), axis=0, keepdims=True)
            for k in range(top_count)
        ]
        total = sum(chosen)
        gates = [value / total for value in chosen]
        gates_all[direction, tick, 0] = jnp.zeros((8, tokens), F32)
        for k in range(top_count):
            gates_all[direction, tick, 0, k : k + 1, :] = gates[k]
        return chosen, total, gates

    def spread(source, target):
        copies = {}
        for h in range(2):
            for j in relayed(h):
                copies[h, j] = remote(
                    source(h), target(slot_of(h, j)), along(hops[h][0], j)
                )
        return copies

    def send_dense(source, dense):
        return spread(lambda h: source.at[h], lambda slot: dense.at[slot])

    def send_gates(direction, tick):
        held = gates_all.at[direction, tick]
        return spread(lambda h: held.at[0], lambda slot: held.at[1 + slot])

    def pack(direction, tick, h, j, source, send, recv):
        pick = picks[direction, pick_rows(h, j), :]
        count = extent[hops[h][1]]

        def body(h, step, carry):
            at = wide_at(step)
            moved = mm(pick, source[:, at]).astype(BF16)
            for m in range(count):
                part = moved[m * capacity : (m + 1) * capacity]
                if m:
                    send[send_index(h, m, j), :, at] = part
                else:
                    recv[h, block_rows(h, 0, j), at] = part
            return carry

        over_wide(h, body)
        return [
            remote(
                send.at[send_index(h, m, j)],
                recv.at[h, block_rows(h, m, j)],
                along(hops[h][1], m),
            )
            for m in targets(h)
        ]

    def pack_own(direction, tick, source, send, recv):
        copies = []
        for h in range(2):
            copies += pack(direction, tick, h, 0, source.at[h], send, recv)
        return copies

    def pack_relayed(direction, tick, dense, trips, send, recv):
        copies = []
        for h in range(2):
            for j in relayed(h):
                trips[h, j].wait_recv()
                copies += pack(direction, tick, h, j, dense.at[slot_of(h, j)], send, recv)
        return copies

    def give_back(block, ret, product):
        trips = {}
        for h in range(2):

            def body(h, step, carry):
                at = wide_at(step)
                value = product(h, step)
                block[h, :, at] = value
                for j in sources(h):
                    ret[h, ret_rows(h, j, 0), at] = value[block_rows(h, 0, j)]
                return carry

            over_wide(h, body)
            for j in reversed(sources(h)):
                trips[h, j] = [
                    remote(
                        block.at[h, block_rows(h, m, j)],
                        ret.at[h, ret_rows(h, j, m)],
                        along(hops[h][1], -m),
                    )
                    for m in targets(h)
                ]
        return trips

    def project(block, at):
        return mm(block[0], up_w[0:half, at]) + mm(block[1], up_w[half:width, at])

    def expert_forward(block):
        def up_body(step, carry):
            at = narrow_at(step)
            upward = project(block, at)
            hid_buf[:, at] = (upward * jax.nn.sigmoid(upward)).astype(BF16)
            return carry

        lax.fori_loop(0, narrow_count, up_body, 0)

        def product(h, step):
            return mm(hid_buf[...], down_w[:, full_at(h, step)]).astype(BF16)

        return give_back(block, ret_f, product)

    def expert_up(block):
        def body(step, carry):
            at = narrow_at(step)
            up_buf[:, at] = project(block, at)
            return carry

        lax.fori_loop(0, narrow_count, body, 0)

    def expert_backward(block, cot_block, tick):
        def body(step, total):
            at = narrow_at(step)
            grad = mm(cot_block[0], down_w[at, 0:half], NT)
            grad = grad + mm(cot_block[1], down_w[at, half:width], NT)
            upward = up_buf[:, at]
            gate = jax.nn.sigmoid(upward)
            hidden = (upward * gate).astype(BF16).astype(F32)
            hid_buf[:, at] = (grad * gate * (1.0 + upward * (1.0 - gate))).astype(BF16)
            return total + folded(hidden * grad)

        total = lax.fori_loop(0, narrow_count, body, jnp.zeros((rows, LANES), F32))
        ones = jnp.ones((8, LANES), F32)
        trips = []
        for source in range(experts):
            part = total[source * capacity : (source + 1) * capacity]
            target = gate_send if source else gate_ret
            target[tick, source] = jnp.zeros((8, LANES), F32)
            target[tick, source, :, 0:capacity] = mm(ones, part, NT, lax.Precision.HIGHEST)
            if source:
                trips.append(
                    remote(
                        gate_send.at[tick, source],
                        gate_ret.at[tick, source],
                        device(-(source % inner), -(source // inner)),
                    )
                )

        def product(h, step):
            return mm(hid_buf[...], up_w[full_at(h, step), :], NT).astype(BF16)

        return trips, give_back(block, ret_g, product)

    def combine(stack, ret, part, comb, trips):
        copies = {}
        for h in range(2):
            for j in relayed(h):
                arrived(trips[h, j])
                slot = slot_of(h, j)

                def body(h, step, carry, j=j, slot=slot):
                    at = wide_at(step)
                    part[slot, :, at] = mixed(stack, ret, h, j, at).astype(BF16)
                    return carry

                over_wide(h, body)
                copies[h, j] = remote(part.at[slot], comb.at[slot], along(hops[h][0], -j))
        for h in range(2):
            arrived(trips[h, 0])
        return copies

    def relays(total, comb, h, at):
        for j in relayed(h):
            total = total + comb[slot_of(h, j), :, at].astype(F32)
        return total

    def prepare_forward(act):
        def body(h, step, carry):
            at = wide_at(step)
            held_buf[h, :, at] = act[h, :, at].astype(F32) + mixed(stack_f, ret_f, h, 0, at)
            return carry

        for h in range(2):
            over_wide(h, body)

    def finish_forward(act, tick, h, trips):
        arrived([trips[h, j] for j in relayed(h)])

        def body(h, step, carry):
            at = wide_at(step)
            value = relays(held_buf[h, :, at], comb_f, h, at).astype(BF16)
            fwd_out[tick, :, full_at(h, step)] = value
            if tick + 1 < ticks:
                act[h, :, at] = value
            return carry

        over_wide(h, body)

    def logit_grads(tick, ready):
        chosen, total, gates = ready
        ids = ids_all[0, ticks + tick]
        names = names_around()
        slot = slots_of(ids, names, 0)
        line = lax.broadcasted_iota(I32, (LANES, tokens), 0).astype(F32)
        found = [jnp.zeros((1, tokens), F32) for _ in range(top_count)]
        for source in range(experts):
            spot = jnp.where(line == slot[source : source + 1], 1.0, 0.0)
            value = mm(gate_ret[tick, source], spot, NN, lax.Precision.HIGHEST)[0:1]
            for k in range(top_count):
                found[k] = found[k] + jnp.where(
                    ids[k : k + 1] == names[source : source + 1], value, 0.0
                )
        mean = sum(found[k] * gates[k] for k in range(top_count))
        grads = jnp.zeros((16, tokens), F32)
        for k in range(top_count):
            value = (found[k] - mean) / total * chosen[k] * (1.0 - chosen[k])
            grads = grads + jnp.where(ids[k : k + 1] == level, value, 0.0)
        return jnp.concatenate([grads, jnp.zeros((LANES - 16, tokens), F32)], axis=0).T

    def prepare_backward(logit_grad):
        def body(h, step, carry):
            at, full = wide_at(step), full_at(h, step)
            grad = mixed(stack_g, ret_g, h, 0, at)
            routed = routing[:, full].astype(F32)
            for e in range(experts):
                grad = grad + logit_grad[:, e : e + 1] * routed[e : e + 1, :]
            held_buf[h, :, at] = grad
            return carry

        for h in range(2):
            over_wide(h, body)

    def finish_backward(cot, tick, source, inverse, trips):
        def body(h, step, total):
            at, full = wide_at(step), full_at(h, step)
            scaled = relays(held_buf[h, :, at], comb_g, h, at) * gain[:, full]
            held_buf[h, :, at] = scaled
            return total + folded(scaled * source[h, :, at].astype(F32))

        total = jnp.zeros((tokens, LANES), F32)
        for h in range(2):
            arrived([trips[h, j] for j in relayed(h)])
            total = over_wide(h, body, total)
        correction = jnp.sum(total, axis=-1, keepdims=True) / float(width)
        factor = inverse * inverse * inverse * correction

        def last_body(h, step, carry):
            at = wide_at(step)
            values = source[h, :, at].astype(F32)
            result = cot[h, :, at].astype(F32) + inverse * held_buf[h, :, at] - values * factor
            value = result.astype(BF16)
            bwd_out[tick, :, full_at(h, step)] = value
            if tick + 1 < ticks:
                cot[h, :, at] = value
            return carry

        return last_body

    def hop(source, target, entry, tick, direction, h):
        shift = 1 if direction == 0 else -1
        index = 2 * direction + h
        edge = 0 if direction == 0 else sections - 1
        last = sections - 1 - edge
        where = jnp.clip(section + shift, 0, sections - 1)
        copy = pltpu.make_async_remote_copy(
            src_ref=source.at[h],
            dst_ref=target.at[h],
            send_sem=pipe_send.at[tick, index],
            recv_sem=pipe_recv.at[tick, index],
            device_id=(where, me),
            device_id_type=pl.DeviceIdType.MESH,
        )
        fresh = pltpu.make_async_copy(
            entry.at[:, half_at(h)], target.at[h], load_sems.at[6 + index]
        )
        pl.when(section != last)(copy.start)
        pl.when(section == edge)(fresh.start)

        def landed():
            pl.when(section != edge)(copy.wait_recv)
            pl.when(section == edge)(fresh.wait)

        def left():
            pl.when(section != last)(copy.wait_send)

        return landed, left

    for tick in range(ticks):
        for direction, ids in enumerate((fwd_ids, bwd_ids)):
            ids_all[0, direction * ticks + tick] = jnp.full((8, tokens), -1, I32)
            ids_all[0, direction * ticks + tick, 0:top_count, :] = ids[tick]
    routing[...] = jnp.zeros(routing.shape, BF16)
    routing[0:experts, :] = router[...]

    waited(load_cot)
    pl.semaphore_wait(barrier, experts + 1)
    trip_i = spread(lambda h: ids_all.at[0], lambda slot: ids_all.at[1 + slot])
    trip_c = send_dense(cots.at[0], dense_c)
    waited(load_act)
    _, logits_f = normalize(acts.at[0], norm_f)
    trip_f = send_dense(norm_f, dense_f)
    gating(0, 0, logits_f)
    trip_w = send_gates(0, 0)
    waited(load_stored[0])
    inverse_s, logits_s = normalize(stored.at[0], norm_s)
    trip_s = send_dense(norm_s, dense_s.at[0])
    ready_s = gating(1, 0, logits_s)
    trip_v = send_gates(1, 0)
    arrived(trip_i.values())
    make_picks(1, 0)
    make_picks(0, 0)
    pack_f = pack_own(0, 0, norm_f, send_f, recv_f.at[0])
    pack_c = pack_own(1, 0, cots.at[0], send_c, recv_c)
    pack_s = pack_own(1, 0, norm_s, send_s, recv_s.at[0])
    pack_f += pack_relayed(0, 0, dense_f, trip_f, send_f, recv_f.at[0])
    pack_c += pack_relayed(1, 0, dense_c, trip_c, send_c, recv_c)
    pack_s += pack_relayed(1, 0, dense_s.at[0], trip_s, send_s, recv_s.at[0])
    waited([load_up, load_down])

    for tick in range(ticks):
        more = tick + 1 < ticks
        act, cot = acts.at[tick], cots.at[tick]
        inverse, ready = inverse_s, ready_s
        trip_gs = trip_v
        if more:
            waited(load_stored[tick + 1])
            sent(trip_s.values())
            inverse_s, logits_s = normalize(stored.at[tick + 1], norm_s)
            ready_s = gating(1, tick + 1, logits_s)
            make_picks(1, tick + 1)
            make_picks(0, tick + 1)
        arrived(trip_w.values())
        make_stacks(0, tick, stack_f)
        arrived(trip_gs.values())
        make_stacks(1, tick, stack_g)

        arrived(pack_f)
        back_f = expert_forward(recv_f.at[tick])
        arrived(pack_s)
        expert_up(recv_s.at[tick])
        arrived(pack_c)
        trip_x, back_g = expert_backward(recv_s.at[tick], recv_c, tick)
        sent(pack_s)
        sent(trip_f.values())
        sent(trip_c.values())

        def forward_end():
            prepare_forward(act)
            hops = []
            for h in range(2):
                finish_forward(act, tick, h, home_f)
                if more:
                    hops.append(hop(act, acts.at[tick + 1], fwd_entry, tick, 0, h))
            return hops

        def backward_end():
            arrived(trip_x)
            prepare_backward(logit_grads(tick, ready))
            last_body = finish_backward(cot, tick, stored.at[tick], inverse, home_g)
            hops = []
            for h in range(2):
                over_wide(h, last_body)
                if more:
                    hops.append(hop(cot, cots.at[tick + 1], bwd_entry, tick, 1, h))
            return hops

        if more:
            home_f = combine(stack_f, ret_f, norm_f, comb_f, back_f)
            next_s = send_dense(norm_s, dense_s.at[tick + 1])
            trip_v = send_gates(1, tick + 1)
            home_g = combine(stack_g, ret_g, part_g, comb_g, back_g)
            pack_s = pack_own(1, tick + 1, norm_s, send_s, recv_s.at[tick + 1])
            hops_f = forward_end()
            pack_s += pack_relayed(
                1, tick + 1, dense_s.at[tick + 1], next_s, send_s, recv_s.at[tick + 1]
            )
            hops_b = backward_end()
        else:
            home_g = combine(stack_g, ret_g, part_g, comb_g, back_g)
            home_f = combine(stack_f, ret_f, norm_f, comb_f, back_f)
            backward_end()
            forward_end()
        sent(pack_f)
        sent(trip_w.values())
        sent(pack_c)
        if not more:
            sent(trip_s.values())
        sent(trip_gs.values())
        sent(trip_x)
        for trips in (back_f, back_g):
            for copies in trips.values():
                sent(copies)
        sent(home_f.values())
        sent(home_g.values())
        if more:
            for landed, _ in hops_f:
                landed()
            _, logits_f = normalize(acts.at[tick + 1], norm_f)
            trip_f = send_dense(norm_f, dense_f)
            gating(0, tick + 1, logits_f)
            trip_w = send_gates(0, tick + 1)
            pack_f = pack_own(0, tick + 1, norm_f, send_f, recv_f.at[tick + 1])
            for landed, _ in hops_b:
                landed()
            trip_c = send_dense(cots.at[tick + 1], dense_c)
            pack_c = pack_own(1, tick + 1, cots.at[tick + 1], send_c, recv_c)
            pack_f += pack_relayed(0, tick + 1, dense_f, trip_f, send_f, recv_f.at[tick + 1])
            pack_c += pack_relayed(1, tick + 1, dense_c, trip_c, send_c, recv_c)
            for _, left in hops_f + hops_b:
                left()
            trip_s = next_s
    sent(trip_i.values())


def per_device(
    fwd_state,
    bwd_cot,
    saved_inputs,
    fwd_entry,
    bwd_entry,
    fwd_ids,
    bwd_ids,
    norm_gain,
    router,
    up_weight,
    down_weight,
):
    sections = lax.axis_size("pipe")
    experts = lax.axis_size("expert")
    ticks, _, tokens, width = saved_inputs.shape
    top_count = fwd_ids.shape[3]
    hidden_width = up_weight.shape[3]
    capacity = -(-(5 * tokens * top_count // (4 * experts)) // 16) * 16
    rows = experts * capacity
    half = width // 2
    inner, outer = sides(experts)
    near, far = near_count(experts), far_count(experts)
    copies = copy_count(experts, ticks)
    anywhere = pl.BlockSpec(memory_space=pl.ANY)
    close = pl.BlockSpec(memory_space=pltpu.VMEM)
    out = pltpu.VMEM((ticks, tokens, width), BF16)
    row_block = pltpu.VMEM((2, rows, half), BF16)
    tick_block = pltpu.VMEM((ticks, 2, rows, half), BF16)
    token_block = pltpu.VMEM((2, tokens, half), BF16)
    tick_tokens = pltpu.VMEM((ticks, 2, tokens, half), BF16)
    near_block = pltpu.VMEM((near, tokens, half), BF16)
    far_block = pltpu.VMEM((far, capacity, half), BF16)
    stack_block = pltpu.VMEM((2 + near, 2 * tokens, max(inner, outer) * capacity), BF16)
    forward, backward = pl.pallas_call(
        functools.partial(window_kernel, sections, experts, capacity),
        name="relay_window",
        out_shape=(out, out),
        in_specs=[anywhere] * 5 + [close] * 4 + [anywhere] * 2,
        out_specs=(close, close),
        scratch_shapes=[
            pltpu.VMEM((width, hidden_width), BF16),
            pltpu.VMEM((hidden_width, width), BF16),
            tick_tokens,
            tick_tokens,
            tick_tokens,
            token_block,
            token_block,
            near_block,
            pltpu.VMEM((ticks, near, tokens, half), BF16),
            near_block,
            far_block,
            far_block,
            far_block,
            tick_block,
            tick_block,
            row_block,
            row_block,
            row_block,
            near_block,
            near_block,
            near_block,
            pltpu.VMEM((1 + near, 2 * ticks, 8, tokens), I32),
            pltpu.VMEM((2, ticks, 1 + near, 8, tokens), F32),
            pltpu.VMEM((2, 2 * rows, tokens), BF16),
            stack_block,
            stack_block,
            pltpu.VMEM((ticks, experts, 8, LANES), F32),
            pltpu.VMEM((ticks, experts, 8, LANES), F32),
            pltpu.VMEM((16, width), BF16),
            pltpu.VMEM((rows, hidden_width), F32),
            pltpu.VMEM((rows, hidden_width), BF16),
            pltpu.VMEM((2, tokens, half), F32),
            pltpu.SemaphoreType.DMA((10 + 2 * ticks,)),
            pltpu.SemaphoreType.DMA((copies,)),
            pltpu.SemaphoreType.DMA((copies,)),
            pltpu.SemaphoreType.DMA((ticks, 4)),
            pltpu.SemaphoreType.DMA((ticks, 4)),
        ],
        compiler_params=pltpu.CompilerParams(
            collective_id=0, has_side_effects=True, vmem_limit_bytes=60 * 1024 * 1024
        ),
    )(
        fwd_state[0],
        bwd_cot[0],
        saved_inputs[:, 0],
        fwd_entry,
        bwd_entry,
        jnp.swapaxes(fwd_ids[:, 0], 1, 2),
        jnp.swapaxes(bwd_ids[:, 0], 1, 2),
        norm_gain,
        router[0].T,
        up_weight[0, 0],
        down_weight[0, 0],
    )
    return forward[:, None], backward[:, None]


def solution(mesh):
    placed = (
        P("pipe", "expert", None),
        P("pipe", "expert", None),
        P(None, "pipe", "expert", None),
        P("expert", None),
        P("expert", None),
        P(None, "pipe", "expert", None),
        P(None, "pipe", "expert", None),
        P("pipe", None),
        P("pipe", None, None),
        P("pipe", "expert", None, None),
        P("pipe", "expert", None, None),
    )
    return jax.shard_map(
        per_device,
        mesh=mesh,
        in_specs=placed,
        out_specs=(P(None, "pipe", "expert", None), P(None, "pipe", "expert", None)),
        check_vma=False,
    )
```

```python
import functools

import jax
import jax.numpy as jnp
from jax import lax
from jax.experimental import pallas as pl
from jax.experimental.pallas import tpu as pltpu
from jax.sharding import PartitionSpec as P

EPSILON = 1e-06
LANES = 128
F32 = jnp.float32
BF16 = jnp.bfloat16
I32 = jnp.int32
NN = (((1,), (0,)), ((), ()))
NT = (((1,), (1,)), ((), ()))


def mm(a, b, dims=NN, precision=None):
    return lax.dot_general(a, b, dims, preferred_element_type=F32, precision=precision)


def tile_of(extent, most):
    size = most
    while extent % size:
        size -= LANES
    return size


def sides(experts):
    inner = 2 if experts % 2 == 0 else 1
    return inner, experts // inner


def hops_of(experts):
    inner, outer = sides(experts)
    return ((0, 1), (1, 0)) if inner == outer else ((0, 1), (0, 1))


def near_count(experts):
    extent = sides(experts)
    return sum(extent[first] - 1 for first, _ in hops_of(experts))


def far_count(experts):
    extent = sides(experts)
    return sum((extent[second] - 1) * extent[first] for first, second in hops_of(experts))


def copy_count(experts, ticks):
    near, far = near_count(experts), far_count(experts)
    return ticks * (7 * near + 5 * far + experts - 1) + near


def window_kernel(
    sections,
    experts,
    capacity,
    fwd_state,
    bwd_cot,
    saved,
    fwd_entry,
    bwd_entry,
    fwd_ids,
    bwd_ids,
    gain,
    router,
    up_hbm,
    down_hbm,
    fwd_out,
    bwd_out,
    up_w,
    down_w,
    acts,
    cots,
    stored,
    norm_f,
    norm_s,
    dense_f,
    dense_s,
    dense_c,
    send_f,
    send_s,
    send_c,
    recv_f,
    recv_s,
    recv_c,
    ret_f,
    ret_g,
    part_g,
    comb_f,
    comb_g,
    ids_all,
    gates_all,
    picks,
    stack_f,
    stack_g,
    gate_send,
    gate_ret,
    routing,
    up_buf,
    hid_buf,
    held_buf,
    load_sems,
    send_sems,
    recv_sems,
    pipe_send,
    pipe_recv,
):
    ticks, tokens, width = saved.shape
    half = width // 2
    top_count = fwd_ids.shape[1]
    hidden_width = up_w.shape[1]
    rows = experts * capacity
    section = lax.axis_index("pipe")
    me = lax.axis_index("expert")
    extent = sides(experts)
    inner, outer = extent
    hops = hops_of(experts)
    lo, hi = lax.rem(me, inner), lax.div(me, inner)
    wide = tile_of(half, 896)
    wide_count = half // wide
    narrow = tile_of(hidden_width, 512)
    narrow_count = hidden_width // narrow

    def half_at(h):
        return slice(h * half, (h + 1) * half)

    def load_rows(source, target, first):
        return [
            pltpu.make_async_copy(
                source.at[:, half_at(h)], target.at[h], load_sems.at[first + h]
            )
            for h in range(2)
        ]

    load_cot = load_rows(bwd_cot, cots.at[0], 0)
    load_act = load_rows(fwd_state, acts.at[0], 2)
    load_up = pltpu.make_async_copy(up_hbm, up_w, load_sems.at[4])
    load_down = pltpu.make_async_copy(down_hbm, down_w, load_sems.at[5])
    load_stored = [load_rows(saved.at[t], stored.at[t], 10 + 2 * t) for t in range(ticks)]
    for load in [*load_cot, *load_stored[0], *load_act, load_up, load_down]:
        load.start()
    for loads in load_stored[1:]:
        for load in loads:
            load.start()

    barrier = pltpu.get_barrier_semaphore()
    for offset in range(1, experts):
        pl.semaphore_signal(
            barrier,
            inc=1,
            device_id=(section, lax.rem(me + offset, experts)),
            device_id_type=pl.DeviceIdType.MESH,
        )
    for offset in (1, sections - 1):
        pl.semaphore_signal(
            barrier,
            inc=1,
            device_id=(lax.rem(section + offset, sections), me),
            device_id_type=pl.DeviceIdType.MESH,
        )

    counter = iter(range(send_sems.shape[0]))

    def remote(source, target, where):
        index = next(counter)
        copy = pltpu.make_async_remote_copy(
            src_ref=source,
            dst_ref=target,
            send_sem=send_sems.at[index],
            recv_sem=recv_sems.at[index],
            device_id=where,
            device_id_type=pl.DeviceIdType.MESH,
        )
        copy.start()
        return copy

    def device(a, b):
        across = lax.rem(hi + b + outer, outer)
        return (section, across * inner + lax.rem(lo + a + inner, inner))

    def along(axis, offset):
        return device(offset, 0) if axis == 0 else device(0, offset)

    def slot_of(h, j):
        return h * (extent[hops[0][0]] - 1) + j - 1

    def block_of(h, m, j):
        a, b = (m, j) if hops[h][0] else (j, m)
        return b * inner + a

    def block_rows(h, m, j):
        block = block_of(h, m, j)
        return slice(block * capacity, (block + 1) * capacity)

    def ret_rows(h, j, m):
        block = j * extent[hops[h][1]] + m
        return slice(block * capacity, (block + 1) * capacity)

    def ret_span(h, j):
        size = extent[hops[h][1]] * capacity
        return slice(j * size, (j + 1) * size)

    def pick_rows(h, j):
        size = extent[hops[h][1]] * capacity
        return slice(h * rows + j * size, h * rows + (j + 1) * size)

    def send_index(h, m, j):
        skipped = (extent[hops[0][1]] - 1) * extent[hops[0][0]]
        return h * skipped + (m - 1) * extent[hops[h][0]] + j

    def stack_index(h, j):
        return h * extent[hops[0][0]] + j

    def sources(h):
        return range(extent[hops[h][0]])

    def targets(h):
        return range(1, extent[hops[h][1]])

    def relayed(h):
        return range(1, extent[hops[h][0]])

    def waited(copies):
        for copy in copies:
            copy.wait()

    def arrived(copies):
        for copy in copies:
            copy.wait_recv()

    def sent(copies):
        for copy in copies:
            copy.wait_send()

    def wide_at(step):
        return pl.ds(pl.multiple_of(step * wide, LANES), wide)

    def full_at(h, step):
        return pl.ds(pl.multiple_of(h * half + step * wide, LANES), wide)

    def narrow_at(step):
        return pl.ds(pl.multiple_of(step * narrow, LANES), narrow)

    def folded(value):
        return sum(value[:, i : i + LANES] for i in range(0, value.shape[1], LANES))

    def over_wide(h, body, carry=0):
        return lax.fori_loop(0, wide_count, functools.partial(body, h), carry)

    before = lax.broadcasted_iota(I32, (tokens, tokens), 0)
    after = lax.broadcasted_iota(I32, (tokens, tokens), 1)
    upper = jnp.where(before < after, 1.0, 0.0).astype(BF16)
    level = lax.broadcasted_iota(I32, (16, tokens), 0)

    def names_along(axis):
        if axis == 0:
            named = hi * inner + lax.rem(lo + level, inner)
        else:
            named = lax.rem(hi + level, outer) * inner + lo
        return jnp.where(level < extent[axis], named, -1)

    def names_around():
        across = lax.rem(hi + lax.div(level, inner), outer)
        named = across * inner + lax.rem(lo + lax.rem(level, inner), inner)
        return jnp.where(level < experts, named, -1)

    def slots_of(ids, names, step):
        member = sum(jnp.where(ids[k : k + 1] == names, 1.0, 0.0) for k in range(top_count))
        position = mm(member.astype(BF16), upper)
        base = level.astype(F32) * float(step)
        return jnp.where(member > 0.5, position + base, -1.0)

    def placed(slot, count, weight=None):
        line = lax.broadcasted_iota(I32, (count * capacity, tokens), 0).astype(F32)
        return sum(
            jnp.where(
                line == slot[m : m + 1, :], 1.0 if weight is None else weight[m : m + 1, :], 0.0
            )
            for m in range(count)
        )

    def ids_of(direction, tick, h, j):
        return ids_all[0 if j == 0 else 1 + slot_of(h, j), direction * ticks + tick]

    def make_picks(direction, tick):
        for h in range(2):
            second = hops[h][1]
            for j in sources(h):
                slot = slots_of(ids_of(direction, tick, h, j), names_along(second), capacity)
                picks[direction, pick_rows(h, j), :] = placed(slot, extent[second]).astype(
                    BF16
                )

    def make_stacks(direction, tick, stack):
        for h in range(2):
            second = hops[h][1]
            count = extent[second]
            for j in sources(h):
                ids = ids_of(direction, tick, h, j)
                gates = gates_all[direction, tick, 0 if j == 0 else 1 + slot_of(h, j)]
                names = names_along(second)
                slot = slots_of(ids, names, capacity)
                weight = sum(
                    jnp.where(ids[k : k + 1] == names, gates[k : k + 1], 0.0)
                    for k in range(top_count)
                )
                matrix = placed(slot, count, weight).T
                high = matrix.astype(BF16)
                low = (matrix - high.astype(F32)).astype(BF16)
                at = stack_index(h, j)
                stack[at, 0:tokens, 0 : count * capacity] = high
                stack[at, tokens : 2 * tokens, 0 : count * capacity] = low

    def mixed(stack, ret, h, j, at):
        size = extent[hops[h][1]] * capacity
        both = mm(stack[stack_index(h, j), :, 0:size], ret[h, ret_span(h, j), at])
        return both[:tokens] + both[tokens:]

    def inverse_of(act):
        def body(h, step, total):
            values = act[h, :, wide_at(step)].astype(F32)
            return total + folded(values * values)

        total = jnp.zeros((tokens, LANES), F32)
        for h in range(2):
            total = over_wide(h, body, total)
        mean = jnp.sum(total, axis=-1, keepdims=True) / float(width)
        return lax.rsqrt(mean + EPSILON)

    def normalize(act, target):
        inverse = inverse_of(act)

        def body(h, step, logits):
            at, full = wide_at(step), full_at(h, step)
            normed = (act[h, :, at].astype(F32) * inverse * gain[:, full]).astype(BF16)
            target[h, :, at] = normed
            return logits + mm(routing[:, full], normed, NT)

        logits = jnp.zeros((16, tokens), F32)
        for h in range(2):
            logits = over_wide(h, body, logits)
        return inverse, logits

    def gating(direction, tick, logits):
        ids = ids_all[0, direction * ticks + tick]
        probability = jax.nn.sigmoid(logits)
        chosen = [
            jnp.sum(jnp.where(ids[k : k + 1] == level, probability, 0.0), axis=0, keepdims=True)
            for k in range(top_count)
        ]
        total = sum(chosen)
        gates = [value / total for value in chosen]
        gates_all[direction, tick, 0] = jnp.zeros((8, tokens), F32)
        for k in range(top_count):
            gates_all[direction, tick, 0, k : k + 1, :] = gates[k]
        return chosen, total, gates

    def spread(source, target):
        copies = {}
        for h in range(2):
            for j in relayed(h):
                copies[h, j] = remote(
                    source(h), target(slot_of(h, j)), along(hops[h][0], j)
                )
        return copies

    def send_dense(source, dense):
        return spread(lambda h: source.at[h], lambda slot: dense.at[slot])

    def send_gates(direction, tick):
        held = gates_all.at[direction, tick]
        return spread(lambda h: held.at[0], lambda slot: held.at[1 + slot])

    def pack(direction, tick, h, j, source, send, recv):
        pick = picks[direction, pick_rows(h, j), :]
        count = extent[hops[h][1]]

        def body(h, step, carry):
            at = wide_at(step)
            moved = mm(pick, source[:, at]).astype(BF16)
            for m in range(count):
                part = moved[m * capacity : (m + 1) * capacity]
                if m:
                    send[send_index(h, m, j), :, at] = part
                else:
                    recv[h, block_rows(h, 0, j), at] = part
            return carry

        over_wide(h, body)
        return [
            remote(
                send.at[send_index(h, m, j)],
                recv.at[h, block_rows(h, m, j)],
                along(hops[h][1], m),
            )
            for m in targets(h)
        ]

    def pack_own(direction, tick, source, send, recv):
        copies = []
        for h in range(2):
            copies += pack(direction, tick, h, 0, source.at[h], send, recv)
        return copies

    def pack_relayed(direction, tick, dense, trips, send, recv):
        copies = []
        for h in range(2):
            for j in relayed(h):
                trips[h, j].wait_recv()
                copies += pack(direction, tick, h, j, dense.at[slot_of(h, j)], send, recv)
        return copies

    def give_back(block, ret, product):
        trips = {}
        for h in range(2):

            def body(h, step, carry):
                at = wide_at(step)
                value = product(h, step)
                block[h, :, at] = value
                for j in sources(h):
                    ret[h, ret_rows(h, j, 0), at] = value[block_rows(h, 0, j)]
                return carry

            over_wide(h, body)
            for j in reversed(sources(h)):
                trips[h, j] = [
                    remote(
                        block.at[h, block_rows(h, m, j)],
                        ret.at[h, ret_rows(h, j, m)],
                        along(hops[h][1], -m),
                    )
                    for m in targets(h)
                ]
        return trips

    def project(block, at):
        return mm(block[0], up_w[0:half, at]) + mm(block[1], up_w[half:width, at])

    def expert_forward(block):
        def up_body(step, carry):
            at = narrow_at(step)
            upward = project(block, at)
            hid_buf[:, at] = (upward * jax.nn.sigmoid(upward)).astype(BF16)
            return carry

        lax.fori_loop(0, narrow_count, up_body, 0)

        def product(h, step):
            return mm(hid_buf[...], down_w[:, full_at(h, step)]).astype(BF16)

        return give_back(block, ret_f, product)

    def expert_up(block):
        def body(step, carry):
            at = narrow_at(step)
            up_buf[:, at] = project(block, at)
            return carry

        lax.fori_loop(0, narrow_count, body, 0)

    def expert_backward(block, cot_block, tick):
        def body(step, total):
            at = narrow_at(step)
            grad = mm(cot_block[0], down_w[at, 0:half], NT)
            grad = grad + mm(cot_block[1], down_w[at, half:width], NT)
            upward = up_buf[:, at]
            gate = jax.nn.sigmoid(upward)
            hidden = (upward * gate).astype(BF16).astype(F32)
            hid_buf[:, at] = (grad * gate * (1.0 + upward * (1.0 - gate))).astype(BF16)
            return total + folded(hidden * grad)

        total = lax.fori_loop(0, narrow_count, body, jnp.zeros((rows, LANES), F32))
        ones = jnp.ones((8, LANES), F32)
        trips = []
        for source in range(experts):
            part = total[source * capacity : (source + 1) * capacity]
            target = gate_send if source else gate_ret
            target[tick, source] = jnp.zeros((8, LANES), F32)
            target[tick, source, :, 0:capacity] = mm(ones, part, NT, lax.Precision.HIGHEST)
            if source:
                trips.append(
                    remote(
                        gate_send.at[tick, source],
                        gate_ret.at[tick, source],
                        device(-(source % inner), -(source // inner)),
                    )
                )

        def product(h, step):
            return mm(hid_buf[...], up_w[full_at(h, step), :], NT).astype(BF16)

        return trips, give_back(block, ret_g, product)

    def combine(stack, ret, part, comb, trips):
        copies = {}
        for h in range(2):
            for j in relayed(h):
                arrived(trips[h, j])
                slot = slot_of(h, j)

                def body(h, step, carry, j=j, slot=slot):
                    at = wide_at(step)
                    part[slot, :, at] = mixed(stack, ret, h, j, at).astype(BF16)
                    return carry

                over_wide(h, body)
                copies[h, j] = remote(part.at[slot], comb.at[slot], along(hops[h][0], -j))
        for h in range(2):
            arrived(trips[h, 0])
        return copies

    def relays(total, comb, h, at):
        for j in relayed(h):
            total = total + comb[slot_of(h, j), :, at].astype(F32)
        return total

    def prepare_forward(act):
        def body(h, step, carry):
            at = wide_at(step)
            held_buf[h, :, at] = act[h, :, at].astype(F32) + mixed(stack_f, ret_f, h, 0, at)
            return carry

        for h in range(2):
            over_wide(h, body)

    def finish_forward(act, tick, h, trips):
        arrived([trips[h, j] for j in relayed(h)])

        def body(h, step, carry):
            at = wide_at(step)
            value = relays(held_buf[h, :, at], comb_f, h, at).astype(BF16)
            fwd_out[tick, :, full_at(h, step)] = value
            if tick + 1 < ticks:
                act[h, :, at] = value
            return carry

        over_wide(h, body)

    def logit_grads(tick, ready):
        chosen, total, gates = ready
        ids = ids_all[0, ticks + tick]
        names = names_around()
        slot = slots_of(ids, names, 0)
        line = lax.broadcasted_iota(I32, (LANES, tokens), 0).astype(F32)
        found = [jnp.zeros((1, tokens), F32) for _ in range(top_count)]
        for source in range(experts):
            spot = jnp.where(line == slot[source : source + 1], 1.0, 0.0)
            value = mm(gate_ret[tick, source], spot, NN, lax.Precision.HIGHEST)[0:1]
            for k in range(top_count):
                found[k] = found[k] + jnp.where(
                    ids[k : k + 1] == names[source : source + 1], value, 0.0
                )
        mean = sum(found[k] * gates[k] for k in range(top_count))
        grads = jnp.zeros((16, tokens), F32)
        for k in range(top_count):
            value = (found[k] - mean) / total * chosen[k] * (1.0 - chosen[k])
            grads = grads + jnp.where(ids[k : k + 1] == level, value, 0.0)
        return jnp.concatenate([grads, jnp.zeros((LANES - 16, tokens), F32)], axis=0).T

    def prepare_backward(logit_grad):
        def body(h, step, carry):
            at, full = wide_at(step), full_at(h, step)
            grad = mixed(stack_g, ret_g, h, 0, at)
            routed = routing[:, full].astype(F32)
            for e in range(experts):
                grad = grad + logit_grad[:, e : e + 1] * routed[e : e + 1, :]
            held_buf[h, :, at] = grad
            return carry

        for h in range(2):
            over_wide(h, body)

    def finish_backward(cot, tick, source, inverse, trips):
        def body(h, step, total):
            at, full = wide_at(step), full_at(h, step)
            scaled = relays(held_buf[h, :, at], comb_g, h, at) * gain[:, full]
            held_buf[h, :, at] = scaled
            return total + folded(scaled * source[h, :, at].astype(F32))

        total = jnp.zeros((tokens, LANES), F32)
        for h in range(2):
            arrived([trips[h, j] for j in relayed(h)])
            total = over_wide(h, body, total)
        correction = jnp.sum(total, axis=-1, keepdims=True) / float(width)
        factor = inverse * inverse * inverse * correction

        def last_body(h, step, carry):
            at = wide_at(step)
            values = source[h, :, at].astype(F32)
            result = cot[h, :, at].astype(F32) + inverse * held_buf[h, :, at] - values * factor
            value = result.astype(BF16)
            bwd_out[tick, :, full_at(h, step)] = value
            if tick + 1 < ticks:
                cot[h, :, at] = value
            return carry

        return last_body

    def hop(source, target, entry, tick, direction, h):
        shift = 1 if direction == 0 else -1
        index = 2 * direction + h
        edge = 0 if direction == 0 else sections - 1
        last = sections - 1 - edge
        where = jnp.clip(section + shift, 0, sections - 1)
        copy = pltpu.make_async_remote_copy(
            src_ref=source.at[h],
            dst_ref=target.at[h],
            send_sem=pipe_send.at[tick, index],
            recv_sem=pipe_recv.at[tick, index],
            device_id=(where, me),
            device_id_type=pl.DeviceIdType.MESH,
        )
        fresh = pltpu.make_async_copy(
            entry.at[:, half_at(h)], target.at[h], load_sems.at[6 + index]
        )
        pl.when(section != last)(copy.start)
        pl.when(section == edge)(fresh.start)

        def landed():
            pl.when(section != edge)(copy.wait_recv)
            pl.when(section == edge)(fresh.wait)

        def left():
            pl.when(section != last)(copy.wait_send)

        return landed, left

    waited(load_cot)
    pl.semaphore_wait(barrier, experts + 1)
    trip_c = send_dense(cots.at[0], dense_c)
    for tick in range(ticks):
        for direction, ids in enumerate((fwd_ids, bwd_ids)):
            ids_all[0, direction * ticks + tick] = jnp.full((8, tokens), -1, I32)
            ids_all[0, direction * ticks + tick, 0:top_count, :] = ids[tick]
    routing[...] = jnp.zeros(routing.shape, BF16)
    routing[0:experts, :] = router[...]
    trip_i = spread(lambda h: ids_all.at[0], lambda slot: ids_all.at[1 + slot])
    waited(load_act)
    _, logits_f = normalize(acts.at[0], norm_f)
    trip_f = send_dense(norm_f, dense_f)
    gating(0, 0, logits_f)
    trip_w = send_gates(0, 0)
    waited(load_stored[0])
    inverse_s, logits_s = normalize(stored.at[0], norm_s)
    trip_s = send_dense(norm_s, dense_s.at[0])
    ready_s = gating(1, 0, logits_s)
    trip_v = send_gates(1, 0)
    arrived(trip_i.values())
    make_picks(1, 0)
    make_picks(0, 0)
    pack_f = pack_own(0, 0, norm_f, send_f, recv_f.at[0])
    pack_f += pack_relayed(0, 0, dense_f, trip_f, send_f, recv_f.at[0])
    pack_s = pack_own(1, 0, norm_s, send_s, recv_s.at[0])
    pack_c = pack_own(1, 0, cots.at[0], send_c, recv_c)
    pack_s += pack_relayed(1, 0, dense_s.at[0], trip_s, send_s, recv_s.at[0])
    pack_c += pack_relayed(1, 0, dense_c, trip_c, send_c, recv_c)
    waited([load_up, load_down])

    for tick in range(ticks):
        more = tick + 1 < ticks
        act, cot = acts.at[tick], cots.at[tick]
        inverse, ready = inverse_s, ready_s
        trip_gs = trip_v
        if more:
            waited(load_stored[tick + 1])
            sent(trip_s.values())
            inverse_s, logits_s = normalize(stored.at[tick + 1], norm_s)
            ready_s = gating(1, tick + 1, logits_s)
            make_picks(1, tick + 1)
            make_picks(0, tick + 1)
        arrived(trip_w.values())
        make_stacks(0, tick, stack_f)
        arrived(trip_gs.values())
        make_stacks(1, tick, stack_g)

        arrived(pack_f)
        back_f = expert_forward(recv_f.at[tick])
        arrived(pack_s)
        expert_up(recv_s.at[tick])
        arrived(pack_c)
        trip_x, back_g = expert_backward(recv_s.at[tick], recv_c, tick)
        sent(pack_s)
        sent(trip_f.values())
        sent(trip_c.values())

        def forward_end():
            prepare_forward(act)
            hops = []
            for h in range(2):
                finish_forward(act, tick, h, home_f)
                if more:
                    hops.append(hop(act, acts.at[tick + 1], fwd_entry, tick, 0, h))
            return hops

        def backward_end():
            arrived(trip_x)
            prepare_backward(logit_grads(tick, ready))
            last_body = finish_backward(cot, tick, stored.at[tick], inverse, home_g)
            hops = []
            for h in range(2):
                over_wide(h, last_body)
                if more:
                    hops.append(hop(cot, cots.at[tick + 1], bwd_entry, tick, 1, h))
            return hops

        if more:
            home_f = combine(stack_f, ret_f, norm_f, comb_f, back_f)
            next_s = send_dense(norm_s, dense_s.at[tick + 1])
            trip_v = send_gates(1, tick + 1)
            home_g = combine(stack_g, ret_g, part_g, comb_g, back_g)
            pack_s = pack_own(1, tick + 1, norm_s, send_s, recv_s.at[tick + 1])
            hops_f = forward_end()
            pack_s += pack_relayed(
                1, tick + 1, dense_s.at[tick + 1], next_s, send_s, recv_s.at[tick + 1]
            )
            hops_b = backward_end()
        else:
            home_g = combine(stack_g, ret_g, part_g, comb_g, back_g)
            home_f = combine(stack_f, ret_f, norm_f, comb_f, back_f)
            backward_end()
            forward_end()
        sent(pack_f)
        sent(trip_w.values())
        sent(pack_c)
        if not more:
            sent(trip_s.values())
        sent(trip_gs.values())
        sent(trip_x)
        for trips in (back_f, back_g):
            for copies in trips.values():
                sent(copies)
        sent(home_f.values())
        sent(home_g.values())
        if more:
            for landed, _ in hops_f:
                landed()
            _, logits_f = normalize(acts.at[tick + 1], norm_f)
            trip_f = send_dense(norm_f, dense_f)
            gating(0, tick + 1, logits_f)
            trip_w = send_gates(0, tick + 1)
            pack_f = pack_own(0, tick + 1, norm_f, send_f, recv_f.at[tick + 1])
            for landed, _ in hops_b:
                landed()
            trip_c = send_dense(cots.at[tick + 1], dense_c)
            pack_c = pack_own(1, tick + 1, cots.at[tick + 1], send_c, recv_c)
            pack_f += pack_relayed(0, tick + 1, dense_f, trip_f, send_f, recv_f.at[tick + 1])
            pack_c += pack_relayed(1, tick + 1, dense_c, trip_c, send_c, recv_c)
            for _, left in hops_f + hops_b:
                left()
            trip_s = next_s
    sent(trip_i.values())


def per_device(
    fwd_state,
    bwd_cot,
    saved_inputs,
    fwd_entry,
    bwd_entry,
    fwd_ids,
    bwd_ids,
    norm_gain,
    router,
    up_weight,
    down_weight,
):
    sections = lax.axis_size("pipe")
    experts = lax.axis_size("expert")
    ticks, _, tokens, width = saved_inputs.shape
    top_count = fwd_ids.shape[3]
    hidden_width = up_weight.shape[3]
    capacity = -(-(5 * tokens * top_count // (4 * experts)) // 16) * 16
    rows = experts * capacity
    half = width // 2
    inner, outer = sides(experts)
    near, far = near_count(experts), far_count(experts)
    copies = copy_count(experts, ticks)
    anywhere = pl.BlockSpec(memory_space=pl.ANY)
    close = pl.BlockSpec(memory_space=pltpu.VMEM)
    out = pltpu.VMEM((ticks, tokens, width), BF16)
    row_block = pltpu.VMEM((2, rows, half), BF16)
    tick_block = pltpu.VMEM((ticks, 2, rows, half), BF16)
    token_block = pltpu.VMEM((2, tokens, half), BF16)
    tick_tokens = pltpu.VMEM((ticks, 2, tokens, half), BF16)
    near_block = pltpu.VMEM((near, tokens, half), BF16)
    far_block = pltpu.VMEM((far, capacity, half), BF16)
    stack_block = pltpu.VMEM((2 + near, 2 * tokens, max(inner, outer) * capacity), BF16)
    forward, backward = pl.pallas_call(
        functools.partial(window_kernel, sections, experts, capacity),
        name="relay_window",
        out_shape=(out, out),
        in_specs=[anywhere] * 5 + [close] * 4 + [anywhere] * 2,
        out_specs=(close, close),
        scratch_shapes=[
            pltpu.VMEM((width, hidden_width), BF16),
            pltpu.VMEM((hidden_width, width), BF16),
            tick_tokens,
            tick_tokens,
            tick_tokens,
            token_block,
            token_block,
            near_block,
            pltpu.VMEM((ticks, near, tokens, half), BF16),
            near_block,
            far_block,
            far_block,
            far_block,
            tick_block,
            tick_block,
            row_block,
            row_block,
            row_block,
            near_block,
            near_block,
            near_block,
            pltpu.VMEM((1 + near, 2 * ticks, 8, tokens), I32),
            pltpu.VMEM((2, ticks, 1 + near, 8, tokens), F32),
            pltpu.VMEM((2, 2 * rows, tokens), BF16),
            stack_block,
            stack_block,
            pltpu.VMEM((ticks, experts, 8, LANES), F32),
            pltpu.VMEM((ticks, experts, 8, LANES), F32),
            pltpu.VMEM((16, width), BF16),
            pltpu.VMEM((rows, hidden_width), F32),
            pltpu.VMEM((rows, hidden_width), BF16),
            pltpu.VMEM((2, tokens, half), F32),
            pltpu.SemaphoreType.DMA((10 + 2 * ticks,)),
            pltpu.SemaphoreType.DMA((copies,)),
            pltpu.SemaphoreType.DMA((copies,)),
            pltpu.SemaphoreType.DMA((ticks, 4)),
            pltpu.SemaphoreType.DMA((ticks, 4)),
        ],
        compiler_params=pltpu.CompilerParams(
            collective_id=0, has_side_effects=True, vmem_limit_bytes=60 * 1024 * 1024
        ),
    )(
        fwd_state[0],
        bwd_cot[0],
        saved_inputs[:, 0],
        fwd_entry,
        bwd_entry,
        jnp.swapaxes(fwd_ids[:, 0], 1, 2),
        jnp.swapaxes(bwd_ids[:, 0], 1, 2),
        norm_gain,
        router[0].T,
        up_weight[0, 0],
        down_weight[0, 0],
    )
    return forward[:, None], backward[:, None]


def solution(mesh):
    placed = (
        P("pipe", "expert", None),
        P("pipe", "expert", None),
        P(None, "pipe", "expert", None),
        P("expert", None),
        P("expert", None),
        P(None, "pipe", "expert", None),
        P(None, "pipe", "expert", None),
        P("pipe", None),
        P("pipe", None, None),
        P("pipe", "expert", None, None),
        P("pipe", "expert", None, None),
    )
    return jax.shard_map(
        per_device,
        mesh=mesh,
        in_specs=placed,
        out_specs=(P(None, "pipe", "expert", None), P(None, "pipe", "expert", None)),
        check_vma=False,
    )
```

```python
import functools

import jax
import jax.numpy as jnp
from jax import lax
from jax.experimental import pallas as pl
from jax.experimental.pallas import tpu as pltpu
from jax.sharding import PartitionSpec as P

EPSILON = 1e-06
LANES = 128
F32 = jnp.float32
BF16 = jnp.bfloat16
I32 = jnp.int32
NN = (((1,), (0,)), ((), ()))
NT = (((1,), (1,)), ((), ()))


def mm(a, b, dims=NN, precision=None):
    return lax.dot_general(a, b, dims, preferred_element_type=F32, precision=precision)


def tile_of(extent, most):
    size = most
    while extent % size:
        size -= LANES
    return size


def sides(experts):
    inner = 2 if experts % 2 == 0 else 1
    return inner, experts // inner


def hops_of(experts):
    inner, outer = sides(experts)
    return ((0, 1), (1, 0)) if inner == outer else ((0, 1), (0, 1))


def near_count(experts):
    extent = sides(experts)
    return sum(extent[first] - 1 for first, _ in hops_of(experts))


def far_count(experts):
    extent = sides(experts)
    return sum((extent[second] - 1) * extent[first] for first, second in hops_of(experts))


def copy_count(experts, ticks):
    near, far = near_count(experts), far_count(experts)
    return ticks * (7 * near + 5 * far + experts - 1) + near


def window_kernel(
    sections,
    experts,
    capacity,
    fwd_state,
    bwd_cot,
    saved,
    fwd_entry,
    bwd_entry,
    fwd_ids,
    bwd_ids,
    gain,
    router,
    up_hbm,
    down_hbm,
    fwd_out,
    bwd_out,
    up_w,
    down_w,
    acts,
    cots,
    stored,
    norm_f,
    norm_s,
    dense_f,
    dense_s,
    dense_c,
    send_f,
    send_s,
    send_c,
    recv_f,
    recv_s,
    recv_c,
    ret_f,
    ret_g,
    part_g,
    comb_f,
    comb_g,
    ids_all,
    gates_all,
    picks,
    stack_f,
    stack_g,
    gate_send,
    gate_ret,
    routing,
    up_buf,
    hid_buf,
    held_buf,
    load_sems,
    send_sems,
    recv_sems,
    pipe_send,
    pipe_recv,
):
    ticks, tokens, width = saved.shape
    half = width // 2
    top_count = fwd_ids.shape[1]
    hidden_width = up_w.shape[1]
    rows = experts * capacity
    section = lax.axis_index("pipe")
    me = lax.axis_index("expert")
    extent = sides(experts)
    inner, outer = extent
    hops = hops_of(experts)
    lo, hi = lax.rem(me, inner), lax.div(me, inner)
    wide = tile_of(half, 896)
    wide_count = half // wide
    narrow = tile_of(hidden_width, 512)
    narrow_count = hidden_width // narrow

    def half_at(h):
        return slice(h * half, (h + 1) * half)

    def load_rows(source, target, first):
        return [
            pltpu.make_async_copy(
                source.at[:, half_at(h)], target.at[h], load_sems.at[first + h]
            )
            for h in range(2)
        ]

    load_cot = load_rows(bwd_cot, cots.at[0], 0)
    load_act = load_rows(fwd_state, acts.at[0], 2)
    load_up = pltpu.make_async_copy(up_hbm, up_w, load_sems.at[4])
    load_down = pltpu.make_async_copy(down_hbm, down_w, load_sems.at[5])
    load_stored = [load_rows(saved.at[t], stored.at[t], 10 + 2 * t) for t in range(ticks)]
    for load in [*load_cot, *load_stored[0], *load_act, load_up, load_down]:
        load.start()
    for loads in load_stored[1:]:
        for load in loads:
            load.start()

    barrier = pltpu.get_barrier_semaphore()
    for offset in range(1, experts):
        pl.semaphore_signal(
            barrier,
            inc=1,
            device_id=(section, lax.rem(me + offset, experts)),
            device_id_type=pl.DeviceIdType.MESH,
        )
    for offset in (1, sections - 1):
        pl.semaphore_signal(
            barrier,
            inc=1,
            device_id=(lax.rem(section + offset, sections), me),
            device_id_type=pl.DeviceIdType.MESH,
        )

    counter = iter(range(send_sems.shape[0]))

    def remote(source, target, where):
        index = next(counter)
        copy = pltpu.make_async_remote_copy(
            src_ref=source,
            dst_ref=target,
            send_sem=send_sems.at[index],
            recv_sem=recv_sems.at[index],
            device_id=where,
            device_id_type=pl.DeviceIdType.MESH,
        )
        copy.start()
        return copy

    def device(a, b):
        across = lax.rem(hi + b + outer, outer)
        return (section, across * inner + lax.rem(lo + a + inner, inner))

    def along(axis, offset):
        return device(offset, 0) if axis == 0 else device(0, offset)

    def slot_of(h, j):
        return h * (extent[hops[0][0]] - 1) + j - 1

    def block_of(h, m, j):
        a, b = (m, j) if hops[h][0] else (j, m)
        return b * inner + a

    def block_rows(h, m, j):
        block = block_of(h, m, j)
        return slice(block * capacity, (block + 1) * capacity)

    def ret_rows(h, j, m):
        block = j * extent[hops[h][1]] + m
        return slice(block * capacity, (block + 1) * capacity)

    def ret_span(h, j):
        size = extent[hops[h][1]] * capacity
        return slice(j * size, (j + 1) * size)

    def pick_rows(h, j):
        size = extent[hops[h][1]] * capacity
        return slice(h * rows + j * size, h * rows + (j + 1) * size)

    def send_index(h, m, j):
        skipped = (extent[hops[0][1]] - 1) * extent[hops[0][0]]
        return h * skipped + (m - 1) * extent[hops[h][0]] + j

    def stack_index(h, j):
        return h * extent[hops[0][0]] + j

    def sources(h):
        return range(extent[hops[h][0]])

    def targets(h):
        return range(1, extent[hops[h][1]])

    def relayed(h):
        return range(1, extent[hops[h][0]])

    def waited(copies):
        for copy in copies:
            copy.wait()

    def arrived(copies):
        for copy in copies:
            copy.wait_recv()

    def sent(copies):
        for copy in copies:
            copy.wait_send()

    def wide_at(step):
        return pl.ds(pl.multiple_of(step * wide, LANES), wide)

    def full_at(h, step):
        return pl.ds(pl.multiple_of(h * half + step * wide, LANES), wide)

    def narrow_at(step):
        return pl.ds(pl.multiple_of(step * narrow, LANES), narrow)

    def folded(value):
        return sum(value[:, i : i + LANES] for i in range(0, value.shape[1], LANES))

    def over_wide(h, body, carry=0):
        return lax.fori_loop(0, wide_count, functools.partial(body, h), carry)

    before = lax.broadcasted_iota(I32, (tokens, tokens), 0)
    after = lax.broadcasted_iota(I32, (tokens, tokens), 1)
    upper = jnp.where(before < after, 1.0, 0.0).astype(BF16)
    level = lax.broadcasted_iota(I32, (16, tokens), 0)

    def names_along(axis):
        if axis == 0:
            named = hi * inner + lax.rem(lo + level, inner)
        else:
            named = lax.rem(hi + level, outer) * inner + lo
        return jnp.where(level < extent[axis], named, -1)

    def names_around():
        across = lax.rem(hi + lax.div(level, inner), outer)
        named = across * inner + lax.rem(lo + lax.rem(level, inner), inner)
        return jnp.where(level < experts, named, -1)

    def slots_of(ids, names, step):
        member = sum(jnp.where(ids[k : k + 1] == names, 1.0, 0.0) for k in range(top_count))
        position = mm(member.astype(BF16), upper)
        base = level.astype(F32) * float(step)
        return jnp.where(member > 0.5, position + base, -1.0)

    def placed(slot, count, weight=None):
        line = lax.broadcasted_iota(I32, (count * capacity, tokens), 0).astype(F32)
        return sum(
            jnp.where(
                line == slot[m : m + 1, :], 1.0 if weight is None else weight[m : m + 1, :], 0.0
            )
            for m in range(count)
        )

    def ids_of(direction, tick, h, j):
        return ids_all[0 if j == 0 else 1 + slot_of(h, j), direction * ticks + tick]

    def make_picks(direction, tick):
        for h in range(2):
            second = hops[h][1]
            for j in sources(h):
                slot = slots_of(ids_of(direction, tick, h, j), names_along(second), capacity)
                picks[direction, pick_rows(h, j), :] = placed(slot, extent[second]).astype(
                    BF16
                )

    def make_stacks(direction, tick, stack):
        for h in range(2):
            second = hops[h][1]
            count = extent[second]
            for j in sources(h):
                ids = ids_of(direction, tick, h, j)
                gates = gates_all[direction, tick, 0 if j == 0 else 1 + slot_of(h, j)]
                names = names_along(second)
                slot = slots_of(ids, names, capacity)
                weight = sum(
                    jnp.where(ids[k : k + 1] == names, gates[k : k + 1], 0.0)
                    for k in range(top_count)
                )
                matrix = placed(slot, count, weight).T
                high = matrix.astype(BF16)
                low = (matrix - high.astype(F32)).astype(BF16)
                at = stack_index(h, j)
                stack[at, 0:tokens, 0 : count * capacity] = high
                stack[at, tokens : 2 * tokens, 0 : count * capacity] = low

    def mixed(stack, ret, h, j, at):
        size = extent[hops[h][1]] * capacity
        both = mm(stack[stack_index(h, j), :, 0:size], ret[h, ret_span(h, j), at])
        return both[:tokens] + both[tokens:]

    def inverse_of(act):
        def body(h, step, total):
            values = act[h, :, wide_at(step)].astype(F32)
            return total + folded(values * values)

        total = jnp.zeros((tokens, LANES), F32)
        for h in range(2):
            total = over_wide(h, body, total)
        mean = jnp.sum(total, axis=-1, keepdims=True) / float(width)
        return lax.rsqrt(mean + EPSILON)

    def normalize(act, target):
        inverse = inverse_of(act)

        def body(h, step, logits):
            at, full = wide_at(step), full_at(h, step)
            normed = (act[h, :, at].astype(F32) * inverse * gain[:, full]).astype(BF16)
            target[h, :, at] = normed
            return logits + mm(routing[:, full], normed, NT)

        logits = jnp.zeros((16, tokens), F32)
        for h in range(2):
            logits = over_wide(h, body, logits)
        return inverse, logits

    def gating(direction, tick, logits):
        ids = ids_all[0, direction * ticks + tick]
        probability = jax.nn.sigmoid(logits)
        chosen = [
            jnp.sum(jnp.where(ids[k : k + 1] == level, probability, 0.0), axis=0, keepdims=True)
            for k in range(top_count)
        ]
        total = sum(chosen)
        gates = [value / total for value in chosen]
        gates_all[direction, tick, 0] = jnp.zeros((8, tokens), F32)
        for k in range(top_count):
            gates_all[direction, tick, 0, k : k + 1, :] = gates[k]
        return chosen, total, gates

    def spread(source, target):
        copies = {}
        for h in range(2):
            for j in relayed(h):
                copies[h, j] = remote(
                    source(h), target(slot_of(h, j)), along(hops[h][0], j)
                )
        return copies

    def send_dense(source, dense):
        return spread(lambda h: source.at[h], lambda slot: dense.at[slot])

    def send_gates(direction, tick):
        held = gates_all.at[direction, tick]
        return spread(lambda h: held.at[0], lambda slot: held.at[1 + slot])

    def pack(direction, tick, h, j, source, send, recv):
        pick = picks[direction, pick_rows(h, j), :]
        count = extent[hops[h][1]]

        def body(h, step, carry):
            at = wide_at(step)
            moved = mm(pick, source[:, at]).astype(BF16)
            for m in range(count):
                part = moved[m * capacity : (m + 1) * capacity]
                if m:
                    send[send_index(h, m, j), :, at] = part
                else:
                    recv[h, block_rows(h, 0, j), at] = part
            return carry

        over_wide(h, body)
        return [
            remote(
                send.at[send_index(h, m, j)],
                recv.at[h, block_rows(h, m, j)],
                along(hops[h][1], m),
            )
            for m in targets(h)
        ]

    def pack_own(direction, tick, source, send, recv):
        copies = []
        for h in range(2):
            copies += pack(direction, tick, h, 0, source.at[h], send, recv)
        return copies

    def pack_relayed(direction, tick, dense, trips, send, recv):
        copies = []
        for h in range(2):
            for j in relayed(h):
                trips[h, j].wait_recv()
                copies += pack(direction, tick, h, j, dense.at[slot_of(h, j)], send, recv)
        return copies

    def give_back(block, ret, product):
        trips = {}
        for h in range(2):

            def body(h, step, carry):
                at = wide_at(step)
                value = product(h, step)
                block[h, :, at] = value
                for j in sources(h):
                    ret[h, ret_rows(h, j, 0), at] = value[block_rows(h, 0, j)]
                return carry

            over_wide(h, body)
            for j in reversed(sources(h)):
                trips[h, j] = [
                    remote(
                        block.at[h, block_rows(h, m, j)],
                        ret.at[h, ret_rows(h, j, m)],
                        along(hops[h][1], -m),
                    )
                    for m in targets(h)
                ]
        return trips

    def project(block, at):
        return mm(block[0], up_w[0:half, at]) + mm(block[1], up_w[half:width, at])

    def expert_forward(block):
        def up_body(step, carry):
            at = narrow_at(step)
            upward = project(block, at)
            hid_buf[:, at] = (upward * jax.nn.sigmoid(upward)).astype(BF16)
            return carry

        lax.fori_loop(0, narrow_count, up_body, 0, unroll=True)

        def product(h, step):
            return mm(hid_buf[...], down_w[:, full_at(h, step)]).astype(BF16)

        return give_back(block, ret_f, product)

    def expert_up(block):
        def body(step, carry):
            at = narrow_at(step)
            up_buf[:, at] = project(block, at)
            return carry

        lax.fori_loop(0, narrow_count, body, 0, unroll=True)

    def expert_backward(block, cot_block, tick):
        def body(step, total):
            at = narrow_at(step)
            grad = mm(cot_block[0], down_w[at, 0:half], NT)
            grad = grad + mm(cot_block[1], down_w[at, half:width], NT)
            upward = up_buf[:, at]
            gate = jax.nn.sigmoid(upward)
            hidden = (upward * gate).astype(BF16).astype(F32)
            hid_buf[:, at] = (grad * gate * (1.0 + upward * (1.0 - gate))).astype(BF16)
            return total + folded(hidden * grad)

        total = lax.fori_loop(0, narrow_count, body, jnp.zeros((rows, LANES), F32), unroll=True)
        ones = jnp.ones((8, LANES), F32)
        trips = []
        for source in range(experts):
            part = total[source * capacity : (source + 1) * capacity]
            target = gate_send if source else gate_ret
            target[tick, source] = jnp.zeros((8, LANES), F32)
            target[tick, source, :, 0:capacity] = mm(ones, part, NT, lax.Precision.HIGHEST)
            if source:
                trips.append(
                    remote(
                        gate_send.at[tick, source],
                        gate_ret.at[tick, source],
                        device(-(source % inner), -(source // inner)),
                    )
                )

        def product(h, step):
            return mm(hid_buf[...], up_w[full_at(h, step), :], NT).astype(BF16)

        return trips, give_back(block, ret_g, product)

    def combine(stack, ret, part, comb, trips):
        copies = {}
        for h in range(2):
            for j in relayed(h):
                arrived(trips[h, j])
                slot = slot_of(h, j)

                def body(h, step, carry, j=j, slot=slot):
                    at = wide_at(step)
                    part[slot, :, at] = mixed(stack, ret, h, j, at).astype(BF16)
                    return carry

                over_wide(h, body)
                copies[h, j] = remote(part.at[slot], comb.at[slot], along(hops[h][0], -j))
        for h in range(2):
            arrived(trips[h, 0])
        return copies

    def relays(total, comb, h, at):
        for j in relayed(h):
            total = total + comb[slot_of(h, j), :, at].astype(F32)
        return total

    def prepare_forward(act):
        def body(h, step, carry):
            at = wide_at(step)
            held_buf[h, :, at] = act[h, :, at].astype(F32) + mixed(stack_f, ret_f, h, 0, at)
            return carry

        for h in range(2):
            over_wide(h, body)

    def finish_forward(act, tick, h, trips):
        arrived([trips[h, j] for j in relayed(h)])

        def body(h, step, carry):
            at = wide_at(step)
            value = relays(held_buf[h, :, at], comb_f, h, at).astype(BF16)
            fwd_out[tick, :, full_at(h, step)] = value
            if tick + 1 < ticks:
                act[h, :, at] = value
            return carry

        over_wide(h, body)

    def logit_grads(tick, ready):
        chosen, total, gates = ready
        ids = ids_all[0, ticks + tick]
        names = names_around()
        slot = slots_of(ids, names, 0)
        line = lax.broadcasted_iota(I32, (LANES, tokens), 0).astype(F32)
        found = [jnp.zeros((1, tokens), F32) for _ in range(top_count)]
        for source in range(experts):
            spot = jnp.where(line == slot[source : source + 1], 1.0, 0.0)
            value = mm(gate_ret[tick, source], spot, NN, lax.Precision.HIGHEST)[0:1]
            for k in range(top_count):
                found[k] = found[k] + jnp.where(
                    ids[k : k + 1] == names[source : source + 1], value, 0.0
                )
        mean = sum(found[k] * gates[k] for k in range(top_count))
        grads = jnp.zeros((16, tokens), F32)
        for k in range(top_count):
            value = (found[k] - mean) / total * chosen[k] * (1.0 - chosen[k])
            grads = grads + jnp.where(ids[k : k + 1] == level, value, 0.0)
        return jnp.concatenate([grads, jnp.zeros((LANES - 16, tokens), F32)], axis=0).T

    def prepare_backward(logit_grad):
        def body(h, step, carry):
            at, full = wide_at(step), full_at(h, step)
            grad = mixed(stack_g, ret_g, h, 0, at)
            routed = routing[:, full].astype(F32)
            for e in range(experts):
                grad = grad + logit_grad[:, e : e + 1] * routed[e : e + 1, :]
            held_buf[h, :, at] = grad
            return carry

        for h in range(2):
            over_wide(h, body)

    def finish_backward(cot, tick, source, inverse, trips):
        def body(h, step, total):
            at, full = wide_at(step), full_at(h, step)
            scaled = relays(held_buf[h, :, at], comb_g, h, at) * gain[:, full]
            held_buf[h, :, at] = scaled
            return total + folded(scaled * source[h, :, at].astype(F32))

        total = jnp.zeros((tokens, LANES), F32)
        for h in range(2):
            arrived([trips[h, j] for j in relayed(h)])
            total = over_wide(h, body, total)
        correction = jnp.sum(total, axis=-1, keepdims=True) / float(width)
        factor = inverse * inverse * inverse * correction

        def last_body(h, step, carry):
            at = wide_at(step)
            values = source[h, :, at].astype(F32)
            result = cot[h, :, at].astype(F32) + inverse * held_buf[h, :, at] - values * factor
            value = result.astype(BF16)
            bwd_out[tick, :, full_at(h, step)] = value
            if tick + 1 < ticks:
                cot[h, :, at] = value
            return carry

        return last_body

    def hop(source, target, entry, tick, direction, h):
        shift = 1 if direction == 0 else -1
        index = 2 * direction + h
        edge = 0 if direction == 0 else sections - 1
        last = sections - 1 - edge
        where = jnp.clip(section + shift, 0, sections - 1)
        copy = pltpu.make_async_remote_copy(
            src_ref=source.at[h],
            dst_ref=target.at[h],
            send_sem=pipe_send.at[tick, index],
            recv_sem=pipe_recv.at[tick, index],
            device_id=(where, me),
            device_id_type=pl.DeviceIdType.MESH,
        )
        fresh = pltpu.make_async_copy(
            entry.at[:, half_at(h)], target.at[h], load_sems.at[6 + index]
        )
        pl.when(section != last)(copy.start)
        pl.when(section == edge)(fresh.start)

        def landed():
            pl.when(section != edge)(copy.wait_recv)
            pl.when(section == edge)(fresh.wait)

        def left():
            pl.when(section != last)(copy.wait_send)

        return landed, left

    waited(load_cot)
    pl.semaphore_wait(barrier, experts + 1)
    trip_c = send_dense(cots.at[0], dense_c)
    for tick in range(ticks):
        for direction, ids in enumerate((fwd_ids, bwd_ids)):
            ids_all[0, direction * ticks + tick] = jnp.full((8, tokens), -1, I32)
            ids_all[0, direction * ticks + tick, 0:top_count, :] = ids[tick]
    routing[...] = jnp.zeros(routing.shape, BF16)
    routing[0:experts, :] = router[...]
    trip_i = spread(lambda h: ids_all.at[0], lambda slot: ids_all.at[1 + slot])
    waited(load_act)
    _, logits_f = normalize(acts.at[0], norm_f)
    trip_f = send_dense(norm_f, dense_f)
    gating(0, 0, logits_f)
    trip_w = send_gates(0, 0)
    waited(load_stored[0])
    inverse_s, logits_s = normalize(stored.at[0], norm_s)
    trip_s = send_dense(norm_s, dense_s.at[0])
    ready_s = gating(1, 0, logits_s)
    trip_v = send_gates(1, 0)
    arrived(trip_i.values())
    make_picks(1, 0)
    make_picks(0, 0)
    pack_f = pack_own(0, 0, norm_f, send_f, recv_f.at[0])
    pack_f += pack_relayed(0, 0, dense_f, trip_f, send_f, recv_f.at[0])
    pack_s = pack_own(1, 0, norm_s, send_s, recv_s.at[0])
    pack_c = pack_own(1, 0, cots.at[0], send_c, recv_c)
    pack_s += pack_relayed(1, 0, dense_s.at[0], trip_s, send_s, recv_s.at[0])
    pack_c += pack_relayed(1, 0, dense_c, trip_c, send_c, recv_c)
    waited([load_up, load_down])

    for tick in range(ticks):
        more = tick + 1 < ticks
        act, cot = acts.at[tick], cots.at[tick]
        inverse, ready = inverse_s, ready_s
        trip_gs = trip_v
        if more:
            waited(load_stored[tick + 1])
            sent(trip_s.values())
            inverse_s, logits_s = normalize(stored.at[tick + 1], norm_s)
            ready_s = gating(1, tick + 1, logits_s)
            make_picks(1, tick + 1)
            make_picks(0, tick + 1)
        arrived(trip_w.values())
        make_stacks(0, tick, stack_f)
        arrived(trip_gs.values())
        make_stacks(1, tick, stack_g)

        arrived(pack_f)
        back_f = expert_forward(recv_f.at[tick])
        arrived(pack_s)
        expert_up(recv_s.at[tick])
        arrived(pack_c)
        trip_x, back_g = expert_backward(recv_s.at[tick], recv_c, tick)
        sent(pack_s)
        sent(trip_f.values())
        sent(trip_c.values())

        def forward_end():
            prepare_forward(act)
            hops = []
            for h in range(2):
                finish_forward(act, tick, h, home_f)
                if more:
                    hops.append(hop(act, acts.at[tick + 1], fwd_entry, tick, 0, h))
            return hops

        def backward_end():
            arrived(trip_x)
            prepare_backward(logit_grads(tick, ready))
            last_body = finish_backward(cot, tick, stored.at[tick], inverse, home_g)
            hops = []
            for h in range(2):
                over_wide(h, last_body)
                if more:
                    hops.append(hop(cot, cots.at[tick + 1], bwd_entry, tick, 1, h))
            return hops

        if more:
            home_f = combine(stack_f, ret_f, norm_f, comb_f, back_f)
            next_s = send_dense(norm_s, dense_s.at[tick + 1])
            trip_v = send_gates(1, tick + 1)
            home_g = combine(stack_g, ret_g, part_g, comb_g, back_g)
            pack_s = pack_own(1, tick + 1, norm_s, send_s, recv_s.at[tick + 1])
            hops_f = forward_end()
            pack_s += pack_relayed(
                1, tick + 1, dense_s.at[tick + 1], next_s, send_s, recv_s.at[tick + 1]
            )
            hops_b = backward_end()
        else:
            home_g = combine(stack_g, ret_g, part_g, comb_g, back_g)
            home_f = combine(stack_f, ret_f, norm_f, comb_f, back_f)
            backward_end()
            forward_end()
        sent(pack_f)
        sent(trip_w.values())
        sent(pack_c)
        if not more:
            sent(trip_s.values())
        sent(trip_gs.values())
        sent(trip_x)
        for trips in (back_f, back_g):
            for copies in trips.values():
                sent(copies)
        sent(home_f.values())
        sent(home_g.values())
        if more:
            for landed, _ in hops_f:
                landed()
            _, logits_f = normalize(acts.at[tick + 1], norm_f)
            trip_f = send_dense(norm_f, dense_f)
            gating(0, tick + 1, logits_f)
            trip_w = send_gates(0, tick + 1)
            pack_f = pack_own(0, tick + 1, norm_f, send_f, recv_f.at[tick + 1])
            for landed, _ in hops_b:
                landed()
            trip_c = send_dense(cots.at[tick + 1], dense_c)
            pack_c = pack_own(1, tick + 1, cots.at[tick + 1], send_c, recv_c)
            pack_f += pack_relayed(0, tick + 1, dense_f, trip_f, send_f, recv_f.at[tick + 1])
            pack_c += pack_relayed(1, tick + 1, dense_c, trip_c, send_c, recv_c)
            for _, left in hops_f + hops_b:
                left()
            trip_s = next_s
    sent(trip_i.values())


def per_device(
    fwd_state,
    bwd_cot,
    saved_inputs,
    fwd_entry,
    bwd_entry,
    fwd_ids,
    bwd_ids,
    norm_gain,
    router,
    up_weight,
    down_weight,
):
    sections = lax.axis_size("pipe")
    experts = lax.axis_size("expert")
    ticks, _, tokens, width = saved_inputs.shape
    top_count = fwd_ids.shape[3]
    hidden_width = up_weight.shape[3]
    capacity = -(-(5 * tokens * top_count // (4 * experts)) // 16) * 16
    rows = experts * capacity
    half = width // 2
    inner, outer = sides(experts)
    near, far = near_count(experts), far_count(experts)
    copies = copy_count(experts, ticks)
    anywhere = pl.BlockSpec(memory_space=pl.ANY)
    close = pl.BlockSpec(memory_space=pltpu.VMEM)
    out = pltpu.VMEM((ticks, tokens, width), BF16)
    row_block = pltpu.VMEM((2, rows, half), BF16)
    tick_block = pltpu.VMEM((ticks, 2, rows, half), BF16)
    token_block = pltpu.VMEM((2, tokens, half), BF16)
    tick_tokens = pltpu.VMEM((ticks, 2, tokens, half), BF16)
    near_block = pltpu.VMEM((near, tokens, half), BF16)
    far_block = pltpu.VMEM((far, capacity, half), BF16)
    stack_block = pltpu.VMEM((2 + near, 2 * tokens, max(inner, outer) * capacity), BF16)
    forward, backward = pl.pallas_call(
        functools.partial(window_kernel, sections, experts, capacity),
        name="relay_window",
        out_shape=(out, out),
        in_specs=[anywhere] * 5 + [close] * 4 + [anywhere] * 2,
        out_specs=(close, close),
        scratch_shapes=[
            pltpu.VMEM((width, hidden_width), BF16),
            pltpu.VMEM((hidden_width, width), BF16),
            tick_tokens,
            tick_tokens,
            tick_tokens,
            token_block,
            token_block,
            near_block,
            pltpu.VMEM((ticks, near, tokens, half), BF16),
            near_block,
            far_block,
            far_block,
            far_block,
            tick_block,
            tick_block,
            row_block,
            row_block,
            row_block,
            near_block,
            near_block,
            near_block,
            pltpu.VMEM((1 + near, 2 * ticks, 8, tokens), I32),
            pltpu.VMEM((2, ticks, 1 + near, 8, tokens), F32),
            pltpu.VMEM((2, 2 * rows, tokens), BF16),
            stack_block,
            stack_block,
            pltpu.VMEM((ticks, experts, 8, LANES), F32),
            pltpu.VMEM((ticks, experts, 8, LANES), F32),
            pltpu.VMEM((16, width), BF16),
            pltpu.VMEM((rows, hidden_width), F32),
            pltpu.VMEM((rows, hidden_width), BF16),
            pltpu.VMEM((2, tokens, half), F32),
            pltpu.SemaphoreType.DMA((10 + 2 * ticks,)),
            pltpu.SemaphoreType.DMA((copies,)),
            pltpu.SemaphoreType.DMA((copies,)),
            pltpu.SemaphoreType.DMA((ticks, 4)),
            pltpu.SemaphoreType.DMA((ticks, 4)),
        ],
        compiler_params=pltpu.CompilerParams(
            collective_id=0, has_side_effects=True, vmem_limit_bytes=60 * 1024 * 1024
        ),
    )(
        fwd_state[0],
        bwd_cot[0],
        saved_inputs[:, 0],
        fwd_entry,
        bwd_entry,
        jnp.swapaxes(fwd_ids[:, 0], 1, 2),
        jnp.swapaxes(bwd_ids[:, 0], 1, 2),
        norm_gain,
        router[0].T,
        up_weight[0, 0],
        down_weight[0, 0],
    )
    return forward[:, None], backward[:, None]


def solution(mesh):
    placed = (
        P("pipe", "expert", None),
        P("pipe", "expert", None),
        P(None, "pipe", "expert", None),
        P("expert", None),
        P("expert", None),
        P(None, "pipe", "expert", None),
        P(None, "pipe", "expert", None),
        P("pipe", None),
        P("pipe", None, None),
        P("pipe", "expert", None, None),
        P("pipe", "expert", None, None),
    )
    return jax.shard_map(
        per_device,
        mesh=mesh,
        in_specs=placed,
        out_specs=(P(None, "pipe", "expert", None), P(None, "pipe", "expert", None)),
        check_vma=False,
    )
```
